128 devices in a mesh: layer: 64 (over z, y, x_hi, core), rows: 2 (over x_lo).
Axes of the slice: x: 4 (x_hi: 2, x_lo: 2; x = x_hi * 2 + x_lo), y: 4, z: 4, core: 2. Of those that a mesh axis runs over, the one named last changes fastest.
Arguments:
- state_guess: bfloat16 [64, 1, 16, 64, 256], P('layer', None, 'rows'), may hold values from -6 to 6
- adjoint_guess: bfloat16 [64, 1, 16, 64, 256], P('layer', None, 'rows'), may hold values from -6 to 6
- weights: bfloat16 [128, 9, 256, 256], P('layer'), may hold values from -0.125 to 0.125
- net_input: bfloat16 [1, 16, 64, 256], P(None, 'rows'), may hold values from -6 to 6
- final_cotangent: bfloat16 [1, 16, 64, 256], P(None, 'rows'), may hold values from -6 to 6
Outputs:
- states: bfloat16 [64, 1, 16, 64, 256], P('layer', None, 'rows')
- adjoints: bfloat16 [64, 1, 16, 64, 256], P('layer', None, 'rows')
- weight_grad: float32 [128, 9, 256, 256], P('layer', None, None, 'rows')
The draws below stay inside these ranges and needn't reach their ends.
All inputs are finite; a program needn't handle non-finite values.
Results may differ from the reference program's by a relative error of at most 0.012.
Values may be sent and summed in bfloat16 or wider, within the bound.
A program may use at most 64 MiB of HBM per device.

```python
import math
import jax
import jax.numpy as jnp
from jax import lax

C = 256
B = 1
ROWS_DEV = 8
IMG_W = 64
H = 16
BLOCKS = 64
LAYERS = 128
N_ROWS = 2


def steps_of(own_key, extent, split, smallest, high):
    gain = 1.0
    for position, shards_of in split:
        heights = jax.random.uniform(jax.random.fold_in(jax.random.fold_in(own_key, 6), position), (shards_of,), jnp.float32, smallest / len(split), high / len(split))
        gain = gain * jnp.repeat(jnp.exp(heights), extent[position] // shards_of).reshape((-1,) + (1,) * (len(extent) - 1 - position))
    return gain


def scatter_about(stream_key, extent, spread, bound, split=(), kind=jnp.bfloat16):
    factor_of = steps_of(stream_key, extent, split, -0.22, 0.18) if split else 1.0
    values = jax.random.normal(stream_key, extent, jnp.float32) * spread * factor_of
    return jnp.minimum(jnp.maximum(values, -bound), bound).astype(kind)


def setup_inputs(seed: int = 0) -> dict:
    key_list = jax.random.split(jax.random.key(seed), 6)
    state_guess = scatter_about(key_list[0], (BLOCKS, B, H, IMG_W, C), 1.0, 6.0, ((0, 64), (2, 2)))
    adjoint_guess = scatter_about(key_list[1], (BLOCKS, B, H, IMG_W, C), 1.0, 6.0, ((0, 64), (2, 2)))
    weights = scatter_about(key_list[2], (LAYERS, 9, C, C), (9 * C) ** -0.5, 0.125, ((0, 64),))
    net_input = scatter_about(key_list[3], (B, H, IMG_W, C), 1.0, 6.0, ((1, 2),))
    final_cotangent = scatter_about(key_list[4], (B, H, IMG_W, C), 1.0, 6.0, ((1, 2),))
    return {"state_guess": state_guess, "adjoint_guess": adjoint_guess, "weights": weights, "net_input": net_input, "final_cotangent": final_cotangent}


def pad_rows(values):
    return jnp.pad(values, ((0, 0), (1, 1), (0, 0), (0, 0)))

def pad_cols(values):
    return jnp.pad(values, ((0, 0), (0, 0), (1, 1), (0, 0)))

def convolve(padded, kernel):
    widened = pad_cols(padded)
    row_count = padded.shape[1] - 2
    col_count = padded.shape[2]
    channels = kernel.shape[-1]
    summed = jnp.zeros((padded.shape[0] * row_count * col_count, channels), jnp.float32)
    for tap_row in range(3):
        for tap_col in range(3):
            window = widened[:, tap_row:tap_row + row_count, tap_col:tap_col + col_count, :].reshape(-1, channels)
            summed = summed + jnp.dot(window, kernel[tap_row * 3 + tap_col], preferred_element_type=jnp.float32)
    return summed.reshape(padded.shape[0], row_count, col_count, channels)

def convolve_back(padded, kernel):
    widened = pad_cols(padded)
    row_count = padded.shape[1] - 2
    col_count = padded.shape[2]
    channels = kernel.shape[-1]
    summed = jnp.zeros((padded.shape[0] * row_count * col_count, channels), jnp.float32)
    for tap_row in range(3):
        for tap_col in range(3):
            window = widened[:, 2 - tap_row:2 - tap_row + row_count, 2 - tap_col:2 - tap_col + col_count, :].reshape(-1, channels)
            summed = summed + lax.dot_general(window, kernel[tap_row * 3 + tap_col], (((1,), (1,)), ((), ())), preferred_element_type=jnp.float32)
    return summed.reshape(padded.shape[0], row_count, col_count, channels)

def weight_term(padded, delta):
    widened = pad_cols(padded)
    row_count = delta.shape[1]
    col_count = delta.shape[2]
    channels = delta.shape[3]
    flat_delta = delta.reshape(-1, channels)
    taps = []
    for tap_row in range(3):
        for tap_col in range(3):
            window = widened[:, tap_row:tap_row + row_count, tap_col:tap_col + col_count, :].reshape(-1, channels)
            taps.append(lax.dot_general(window, flat_delta, (((0,), (0,)), ((), ())), preferred_element_type=jnp.float32))
    return jnp.stack(taps)

def activation_slope(values):
    sigmoid_value = jax.nn.sigmoid(values)
    return sigmoid_value * (1.0 + values * (1.0 - sigmoid_value))

def advance(state, kernel):
    pre_act = convolve(pad_rows(state), kernel)
    return ((state.astype(jnp.float32) + 0.5 * jax.nn.silu(pre_act)).astype(jnp.bfloat16), pre_act)

def band_grad(padded, delta, grad_scale):
    summed = jnp.zeros((9, delta.shape[3], delta.shape[3]), jnp.float32)
    for band_index in range(N_ROWS):
        low = band_index * ROWS_DEV
        partial_value = weight_term(padded[:, low:low + ROWS_DEV + 2], delta[:, low:low + ROWS_DEV]) * grad_scale
        summed = summed + partial_value.astype(jnp.bfloat16).astype(jnp.float32)
    return summed

def reference(state_guess, adjoint_guess, weights, net_input, final_cotangent):
    channels = weights.shape[-1]
    kernel_pairs = weights.reshape(BLOCKS, 2, 9, channels, channels)
    grad_scale = 1.0 / math.sqrt(B * H * IMG_W)

    def forward_end(inputs):
        start_state, kernel_pair = inputs
        middle, _ = advance(start_state, kernel_pair[0])
        block_end, _ = advance(middle, kernel_pair[1])
        return block_end
    ends_one = lax.map(forward_end, (state_guess, kernel_pairs))
    sweep_one = jnp.concatenate([net_input[None], ends_one[:-1]], 0)
    ends_two = lax.map(forward_end, (sweep_one, kernel_pairs))
    states = jnp.concatenate([net_input[None], ends_two[:-1]], 0)
    block_ends = jnp.concatenate([adjoint_guess[1:], final_cotangent[None]], 0)

    def backward(inputs):
        start_state, end_adjoint, kernel_pair = inputs
        middle, pre_first = advance(start_state, kernel_pair[0])
        pre_second = convolve(pad_rows(middle), kernel_pair[1])
        end_float = end_adjoint.astype(jnp.float32)
        delta_second = (0.5 * activation_slope(pre_second) * end_float).astype(jnp.bfloat16)
        back_middle = (end_float + convolve_back(pad_rows(delta_second), kernel_pair[1])).astype(jnp.bfloat16)
        delta_first = (0.5 * activation_slope(pre_first) * back_middle.astype(jnp.float32)).astype(jnp.bfloat16)
        adjoint = (back_middle.astype(jnp.float32) + convolve_back(pad_rows(delta_first), kernel_pair[0])).astype(jnp.bfloat16)
        grad_first = band_grad(pad_rows(start_state), delta_first, grad_scale)
        grad_second = band_grad(pad_rows(middle), delta_second, grad_scale)
        return (adjoint, jnp.stack([grad_first, grad_second]))
    adjoints, grads = lax.map(backward, (states, block_ends, kernel_pairs))
    return (states, adjoints, grads.reshape(LAYERS, 9, channels, channels))
```

```python
import math

import jax
import jax.numpy as jnp
from jax import lax
from jax.experimental import pallas as pl
from jax.experimental.pallas import tpu as pltpu
from jax.sharding import PartitionSpec as P

MESH = pl.DeviceIdType.MESH
F32 = jnp.float32
BF16 = jnp.bfloat16
ROWS = 16
BAND = 8
W = 64
C = 256
PX = ROWS * W
BPX = BAND * W


def span(row, count):
    start = (row + 1) * W
    return pl.ds(start if isinstance(start, int) else pl.multiple_of(start, W), count * W)


def flat(row, count):
    start = row * W
    return pl.ds(start if isinstance(start, int) else pl.multiple_of(start, W), count * W)


def conv(src, weights, layer, row, count, back=False):
    n = count * W
    shifted = []
    for b in range(3):
        acc = None
        for a in range(3):
            window = src[span(row + a - 1, count), :]
            if back:
                term = lax.dot_general(
                    window,
                    weights[layer * 9 + (2 - a) * 3 + (2 - b)],
                    (((1,), (1,)), ((), ())),
                    preferred_element_type=F32,
                )
            else:
                term = jnp.dot(window, weights[layer * 9 + a * 3 + b], preferred_element_type=F32)
            acc = term if acc is None else acc + term
        shifted.append(acc)
    col = lax.broadcasted_iota(jnp.int32, (n, C), 0) % W
    left = jnp.where(col == 0, 0.0, pltpu.roll(shifted[0], 1, 0))
    right = jnp.where(col == W - 1, 0.0, pltpu.roll(shifted[2], n - 1, 0))
    return shifted[1] + left + right


def advance(src, dst, weights, layer, row, count, pre=None):
    value = conv(src, weights, layer, row, count)
    state = src[span(row, count), :].astype(F32)
    dst[span(row, count), :] = (state + 0.5 * value / (1.0 + jnp.exp(-value))).astype(BF16)
    if pre is not None:
        pre[flat(row, count), :] = value


def half_slope(value):
    s = 1.0 / (1.0 + jnp.exp(-value))
    return 0.5 * s * (1.0 + value * (1.0 - s))


def sweep_kernel(
    layers,
    guess, adj_guess, weights_hbm, net_input, cotangent,
    states_out, middle_out, delta1_out, delta2_out, adjoint_out,
    weights, x0, x1, x2, mid, mid3, end1, end2, adj, delta2, back, delta1, pre1, adj_own,
    load_sem, send_sem, halo_sem, x1_sem, x2_sem, adj_sem, out_sem,
):
    l = lax.axis_index("layer")
    r = lax.axis_index("rows")
    o = 1 - r
    even = l % 2 == 0
    first = l == 0
    last = l == layers - 1
    up = jnp.minimum(l + 1, layers - 1)
    down = jnp.maximum(l - 1, 0)
    own = r * BAND
    other = o * BAND

    loads = [
        pltpu.make_async_copy(guess, x0.at[span(own, BAND)], load_sem.at[0]),
        pltpu.make_async_copy(weights_hbm.at[pl.ds(0, 9)], weights.at[pl.ds(0, 9)], load_sem.at[1]),
        pltpu.make_async_copy(weights_hbm.at[pl.ds(9, 9)], weights.at[pl.ds(9, 9)], load_sem.at[2]),
    ]
    for copy in loads:
        copy.start()

    barrier = pltpu.get_barrier_semaphore()
    pl.semaphore_signal(barrier, inc=1, device_id=(l, o), device_id_type=MESH)

    @pl.when(jnp.logical_not(first))
    def _():
        pl.semaphore_signal(barrier, inc=1, device_id=(down, r), device_id_type=MESH)
        pl.semaphore_signal(barrier, inc=1, device_id=(down, o), device_id_type=MESH)

    @pl.when(jnp.logical_not(last))
    def _():
        pl.semaphore_signal(barrier, inc=1, device_id=(up, r), device_id_type=MESH)
        pl.semaphore_signal(barrier, inc=1, device_id=(up, o), device_id_type=MESH)

    zero = jnp.zeros((W, C), BF16)
    for buf in (x0, x1, x2, mid, mid3, delta2, delta1):
        buf[pl.ds(0, W), :] = zero
        buf[pl.ds((ROWS + 1) * W, W), :] = zero

    @pl.when(first | last)
    def _():
        pl.semaphore_wait(barrier, 3)

    @pl.when(jnp.logical_not(first | last))
    def _():
        pl.semaphore_wait(barrier, 5)

    def remote(src, dst, send, recv, device):
        return pltpu.make_async_remote_copy(
            src_ref=src, dst_ref=dst, send_sem=send_sem.at[send], recv_sem=recv,
            device_id=device, device_id_type=MESH,
        )

    edge = 6 + 2 * r
    inner1 = 9 * r
    inner2 = 10 * r
    other_edge = 6 + 2 * o

    loads[0].wait()
    halo = remote(x0.at[span(edge, 2)], x0.at[span(edge, 2)], 0, halo_sem.at[0], (l, o))
    halo.start()
    halo_in = remote(x0.at[span(other_edge, 2)], x0.at[span(other_edge, 2)], 0, halo_sem.at[0], (l, o))

    net1 = remote(net_input, x1.at[span(own, BAND)], 1, x1_sem.at[r], (l, o))
    net2 = remote(net_input, x2.at[span(own, BAND)], 2, x2_sem.at[r], (l, o))
    net1_here = pltpu.make_async_copy(net_input, x1.at[span(own, BAND)], x1_sem.at[r])
    net2_here = pltpu.make_async_copy(net_input, x2.at[span(own, BAND)], x2_sem.at[r])
    adj_last = remote(cotangent, adj.at[flat(own, BAND)], 3, adj_sem.at[r], (l, o))
    adj_last_here = pltpu.make_async_copy(cotangent, adj.at[flat(own, BAND)], adj_sem.at[r])
    adj_same = remote(adj_guess, adj.at[flat(own, BAND)], 4, adj_sem.at[r], (down, r))
    adj_cross = remote(adj_guess, adj.at[flat(own, BAND)], 5, adj_sem.at[r], (down, o))

    @pl.when(first)
    def _():
        net1_here.start()
        net1.start()
        net2_here.start()
        net2.start()

    loads[1].wait()
    advance(x0, mid, weights, 0, inner1, 7)
    loads[2].wait()
    advance(mid, end1, weights, 1, inner2, 6)

    def ship(buf, target, rows, count, send, sem, device):
        return remote(buf.at[span(rows, count)], target.at[span(rows, count)], send, sem, device)

    e1_inner_same = ship(end1, x1, inner2, 6, 6, x1_sem.at[r], (up, r))
    e1_inner_cross = ship(end1, x1, inner2, 6, 7, x1_sem.at[r], (up, o))
    e1_edge_same = ship(end1, x1, edge, 2, 8, x1_sem.at[r], (up, r))
    e1_edge_cross = ship(end1, x1, edge, 2, 9, x1_sem.at[r], (up, o))
    passes = jnp.logical_not(last)

    @pl.when(passes)
    def _():
        e1_inner_same.start()

        @pl.when(jnp.logical_not(even))
        def _():
            e1_inner_cross.start()

    halo_in.wait_recv()
    advance(x0, mid, weights, 0, 7, 2)
    advance(mid, end1, weights, 1, edge, 2)

    @pl.when(passes)
    def _():
        e1_edge_same.start()
        e1_edge_cross.start()

    @pl.when(last)
    def _():
        adj_last_here.start()
        adj_last.start()

    @pl.when(jnp.logical_not(first))
    def _():
        adj_same.start()
        adj_cross.start()

    x1_own = ship(end1, x1, own, BAND, 6, x1_sem.at[r], (l, o))
    x1_other = ship(end1, x1, other, BAND, 6, x1_sem.at[o], (l, o))
    x1_edge = ship(end1, x1, other_edge, 2, 6, x1_sem.at[o], (l, o))
    e2_inner_same = ship(end2, x2, inner2, 6, 10, x2_sem.at[r], (up, r))
    e2_inner_cross = ship(end2, x2, inner2, 6, 11, x2_sem.at[r], (up, o))
    e2_edge_same = ship(end2, x2, edge, 2, 12, x2_sem.at[r], (up, r))
    e2_edge_cross = ship(end2, x2, edge, 2, 13, x2_sem.at[r], (up, o))
    e2_low = ship(end2, x2, 0, BAND, 10, x2_sem.at[0], (up, r))
    e2_high = ship(end2, x2, BAND, BAND, 11, x2_sem.at[1], (up, r))

    @pl.when(jnp.logical_not(even))
    def _():
        x1_own.wait_recv()
        advance(x1, mid, weights, 0, inner1, 7)
        advance(mid, end2, weights, 1, inner2, 6)

        @pl.when(passes)
        def _():
            e2_inner_same.start()
            e2_inner_cross.start()

        x1_edge.wait_recv()
        advance(x1, mid, weights, 0, 7, 2)
        advance(mid, end2, weights, 1, edge, 2)

        @pl.when(passes)
        def _():
            e2_edge_same.start()
            e2_edge_cross.start()

    @pl.when(even)
    def _():
        x1_own.wait_recv()
        x1_other.wait_recv()
        advance(x1, mid, weights, 0, 0, ROWS)
        advance(mid, end2, weights, 1, 0, BAND)
        e2_low.start()
        advance(mid, end2, weights, 1, BAND, BAND)
        e2_high.start()

    x2_own = ship(end1, x2, own, BAND, 6, x2_sem.at[r], (l, o))
    x2_other = ship(end1, x2, other, BAND, 6, x2_sem.at[o], (l, o))
    x2_own.wait_recv()
    x2_other.wait_recv()
    outs = [pltpu.make_async_copy(x2.at[span(0, ROWS)], states_out, out_sem.at[0])]
    outs[-1].start()
    advance(x2, mid3, weights, 0, 0, ROWS, pre1)
    outs.append(pltpu.make_async_copy(mid3.at[span(0, ROWS)], middle_out, out_sem.at[1]))
    outs[-1].start()

    value = conv(mid3, weights, 1, 0, ROWS)
    remote(cotangent, adj.at[flat(own, BAND)], 3, adj_sem.at[r], (l, o)).wait_recv()
    remote(cotangent, adj.at[flat(other, BAND)], 3, adj_sem.at[o], (l, o)).wait_recv()
    delta2[span(0, ROWS), :] = (half_slope(value) * adj[...].astype(F32)).astype(BF16)
    half = pl.ds(pl.multiple_of(r * 128, 128), 128)
    outs.append(pltpu.make_async_copy(delta2.at[span(0, ROWS), half], delta2_out, out_sem.at[2]))
    outs[-1].start()

    value = conv(delta2, weights, 1, 0, ROWS, back=True)
    value = (adj[...].astype(F32) + value).astype(BF16)
    back[...] = value
    delta1[span(0, ROWS), :] = (half_slope(pre1[...]) * value.astype(F32)).astype(BF16)
    outs.append(pltpu.make_async_copy(delta1.at[span(0, ROWS), half], delta1_out, out_sem.at[3]))
    outs[-1].start()

    value = conv(delta1, weights, 0, own, BAND, back=True)
    adj_own[...] = (back[flat(own, BAND), :].astype(F32) + value).astype(BF16)
    outs.append(pltpu.make_async_copy(adj_own, adjoint_out, out_sem.at[4]))
    outs[-1].start()

    halo.wait_send()

    @pl.when(first)
    def _():
        net1.wait_send()
        net2.wait_send()

    @pl.when(last)
    def _():
        adj_last.wait_send()

    @pl.when(jnp.logical_not(first))
    def _():
        adj_same.wait_send()
        adj_cross.wait_send()

    @pl.when(passes)
    def _():
        e1_inner_same.wait_send()
        e1_edge_same.wait_send()
        e1_edge_cross.wait_send()

        @pl.when(jnp.logical_not(even))
        def _():
            e1_inner_cross.wait_send()
            e2_inner_same.wait_send()
            e2_inner_cross.wait_send()
            e2_edge_same.wait_send()
            e2_edge_cross.wait_send()

    @pl.when(even)
    def _():
        e2_low.wait_send()
        e2_high.wait_send()

    for copy in outs:
        copy.wait()


def grad_kernel(
    scale,
    states, middle, delta1, delta2, adjoint,
    states_out, adjoint_out, grad_out,
    x, m, d1, d2, wide, grads, sem, out_sem,
):
    r = lax.axis_index("rows")
    loads = [
        pltpu.make_async_copy(middle, m, sem.at[0]),
        pltpu.make_async_copy(delta2, d2, sem.at[1]),
        pltpu.make_async_copy(states, x, sem.at[2]),
        pltpu.make_async_copy(delta1, d1, sem.at[3]),
    ]
    for copy in loads:
        copy.start()
    outs = [
        pltpu.make_async_copy(states.at[flat(r * BAND, BAND)], states_out, out_sem.at[0]),
        pltpu.make_async_copy(adjoint, adjoint_out, out_sem.at[1]),
    ]
    for copy in outs:
        copy.start()
    zero = jnp.zeros((W, 384), BF16)
    for layer in range(2):
        wide[layer, pl.ds(0, W), :] = zero
        wide[layer, pl.ds((ROWS + 1) * W, W), :] = zero
    col = lax.broadcasted_iota(jnp.int32, (PX, 128), 0) % W
    for layer, image, delta, pair in ((1, m, d2, 0), (0, x, d1, 2)):
        loads[pair].wait()
        loads[pair + 1].wait()
        value = delta[...].astype(F32)
        after = jnp.where(col == W - 1, 0.0, pltpu.roll(value, PX - 1, 0))
        before = jnp.where(col == 0, 0.0, pltpu.roll(value, 1, 0))
        wide[layer, pl.ds(W, PX), 0:128] = after.astype(BF16)
        wide[layer, pl.ds(W, PX), 128:256] = delta[...]
        wide[layer, pl.ds(W, PX), 256:384] = before.astype(BF16)
        side = jnp.concatenate([wide[layer, pl.ds((2 - a) * W, PX), :] for a in range(3)], axis=1)
        terms = lax.dot_general(
            image[...], side, (((0,), (0,)), ((), ())), preferred_element_type=F32
        )
        for tap in range(9):
            grads[layer, tap] = terms[:, tap * 128 : (tap + 1) * 128] * scale
        outs.append(pltpu.make_async_copy(grads.at[layer], grad_out.at[layer], out_sem.at[2 + layer]))
        outs[-1].start()
    for copy in outs:
        copy.wait()


def solution(mesh):
    layers = mesh.shape["layer"]
    scale = 1.0 / math.sqrt(PX)
    hbm = pl.BlockSpec(memory_space=pl.ANY)
    image = lambda rows: pltpu.VMEM((rows * W, C), BF16)

    def local(guess, adj_guess, weights, net_input, cotangent):
        args = (
            guess.reshape(BPX, C),
            adj_guess.reshape(BPX, C),
            weights.reshape(18, C, C),
            net_input.reshape(BPX, C),
            cotangent.reshape(BPX, C),
        )
        sds = jax.ShapeDtypeStruct
        states, middle, delta1, delta2, adjoint = pl.pallas_call(
            lambda *refs: sweep_kernel(layers, *refs),
            out_shape=(
                sds((PX, C), BF16), sds((PX, C), BF16), sds((PX, 128), BF16), sds((PX, 128), BF16),
                sds((BPX, C), BF16),
            ),
            in_specs=[hbm] * 5,
            out_specs=[hbm] * 5,
            scratch_shapes=[
                pltpu.VMEM((18, C, C), BF16),
                image(18), image(18), image(18), image(18), image(18), image(18), image(18),
                image(16), image(18), image(16), image(18),
                pltpu.VMEM((PX, C), F32),
                image(8),
                pltpu.SemaphoreType.DMA((3,)),
                pltpu.SemaphoreType.DMA((14,)),
                pltpu.SemaphoreType.DMA((1,)),
                pltpu.SemaphoreType.DMA((2,)),
                pltpu.SemaphoreType.DMA((2,)),
                pltpu.SemaphoreType.DMA((2,)),
                pltpu.SemaphoreType.DMA((5,)),
            ],
            compiler_params=pltpu.CompilerParams(
                collective_id=0, has_side_effects=True, vmem_limit_bytes=48 << 20
            ),
            name="sweeps",
        )(*args)
        states, adjoint, grads = pl.pallas_call(
            lambda *refs: grad_kernel(scale, *refs),
            out_shape=(sds((BPX, C), BF16), sds((BPX, C), BF16), sds((2, 9, C, 128), F32)),
            in_specs=[hbm] * 5,
            out_specs=[hbm] * 3,
            scratch_shapes=[
                image(16), image(16),
                pltpu.VMEM((PX, 128), BF16), pltpu.VMEM((PX, 128), BF16),
                pltpu.VMEM((2, 18 * W, 384), BF16),
                pltpu.VMEM((2, 9, C, 128), F32),
                pltpu.SemaphoreType.DMA((4,)),
                pltpu.SemaphoreType.DMA((4,)),
            ],
            compiler_params=pltpu.CompilerParams(vmem_limit_bytes=48 << 20),
            name="weight_grads",
        )(states, middle, delta1, delta2, adjoint)
        shape = (1, 1, BAND, W, C)
        return states.reshape(shape), adjoint.reshape(shape), grads

    in_specs = (
        P("layer", None, "rows", None, None),
        P("layer", None, "rows", None, None),
        P("layer", None, None, None),
        P(None, "rows", None, None),
        P(None, "rows", None, None),
    )
    out_specs = (
        P("layer", None, "rows", None, None),
        P("layer", None, "rows", None, None),
        P("layer", None, None, "rows"),
    )
    return jax.shard_map(local, mesh=mesh, in_specs=in_specs, out_specs=out_specs, check_vma=False)
```

```python
import math

import jax
import jax.numpy as jnp
from jax import lax
from jax.experimental import pallas as pl
from jax.experimental.pallas import tpu as pltpu
from jax.sharding import PartitionSpec as P

MESH = pl.DeviceIdType.MESH
F32 = jnp.float32
BF16 = jnp.bfloat16
ROWS = 16
BAND = 8
W = 64
C = 256
PX = ROWS * W
BPX = BAND * W


def span(row, count):
    start = (row + 1) * W
    return pl.ds(start if isinstance(start, int) else pl.multiple_of(start, W), count * W)


def flat(row, count):
    start = row * W
    return pl.ds(start if isinstance(start, int) else pl.multiple_of(start, W), count * W)


def conv(src, weights, layer, row, count, back=False):
    n = count * W
    shifted = []
    for b in range(3):
        acc = None
        for a in range(3):
            window = src[span(row + a - 1, count), :]
            if back:
                term = lax.dot_general(
                    window,
                    weights[layer * 9 + (2 - a) * 3 + (2 - b)],
                    (((1,), (1,)), ((), ())),
                    preferred_element_type=F32,
                )
            else:
                term = jnp.dot(window, weights[layer * 9 + a * 3 + b], preferred_element_type=F32)
            acc = term if acc is None else acc + term
        shifted.append(acc)
    col = lax.broadcasted_iota(jnp.int32, (n, C), 0) % W
    left = jnp.where(col == 0, 0.0, pltpu.roll(shifted[0], 1, 0))
    right = jnp.where(col == W - 1, 0.0, pltpu.roll(shifted[2], n - 1, 0))
    return shifted[1] + left + right


def advance(src, dst, weights, layer, row, count, pre=None):
    value = conv(src, weights, layer, row, count)
    state = src[span(row, count), :].astype(F32)
    dst[span(row, count), :] = (state + 0.5 * value / (1.0 + jnp.exp(-value))).astype(BF16)
    if pre is not None:
        pre[flat(row, count), :] = value


def half_slope(value):
    s = 1.0 / (1.0 + jnp.exp(-value))
    return 0.5 * s * (1.0 + value * (1.0 - s))


def sweep_kernel(
    layers,
    guess, adj_guess, weights_hbm, net_input, cotangent,
    states_out, middle_out, delta1_out, delta2_out, adjoint_out,
    weights, x0, x1, x2, mid, mid3, end1, end2, adj, delta2, back, delta1, pre1, pre2, adj_own,
    load_sem, send_sem, halo_sem, x1_sem, x2_sem, adj_sem, out_sem,
):
    l = lax.axis_index("layer")
    r = lax.axis_index("rows")
    o = 1 - r
    even = l % 2 == 0
    odd = l % 2 == 1
    first = l == 0
    last = l == layers - 1
    passes = jnp.logical_not(last)
    takes = jnp.logical_not(first)
    up = jnp.minimum(l + 1, layers - 1)
    down = jnp.maximum(l - 1, 0)
    t = (r + l) % 2
    s = (r + l + 1) % 2
    own = r * BAND
    other = o * BAND

    loads = [
        pltpu.make_async_copy(guess, x0.at[span(own, BAND)], load_sem.at[0]),
        pltpu.make_async_copy(weights_hbm.at[pl.ds(0, 9)], weights.at[pl.ds(0, 9)], load_sem.at[1]),
        pltpu.make_async_copy(weights_hbm.at[pl.ds(9, 9)], weights.at[pl.ds(9, 9)], load_sem.at[2]),
    ]
    for copy in loads:
        copy.start()

    barrier = pltpu.get_barrier_semaphore()
    pl.semaphore_signal(barrier, inc=1, device_id=(l, o), device_id_type=MESH)

    @pl.when(jnp.logical_not(first))
    def _():
        pl.semaphore_signal(barrier, inc=1, device_id=(down, r), device_id_type=MESH)
        pl.semaphore_signal(barrier, inc=1, device_id=(down, o), device_id_type=MESH)

    @pl.when(jnp.logical_not(last))
    def _():
        pl.semaphore_signal(barrier, inc=1, device_id=(up, r), device_id_type=MESH)
        pl.semaphore_signal(barrier, inc=1, device_id=(up, o), device_id_type=MESH)

    zero = jnp.zeros((W, C), BF16)
    for buf in (x0, x1, x2, mid, mid3, delta2, delta1):
        buf[pl.ds(0, W), :] = zero
        buf[pl.ds((ROWS + 1) * W, W), :] = zero

    @pl.when(first | last)
    def _():
        pl.semaphore_wait(barrier, 3)

    @pl.when(jnp.logical_not(first | last))
    def _():
        pl.semaphore_wait(barrier, 5)

    def remote(src, dst, send, recv, device):
        return pltpu.make_async_remote_copy(
            src_ref=src, dst_ref=dst, send_sem=send_sem.at[send], recv_sem=recv,
            device_id=device, device_id_type=MESH,
        )

    edge = lambda band: 6 + 2 * band
    inner = lambda band: 10 * band

    def ship(buf, target, rows, count, send, sem, device):
        return remote(buf.at[span(rows, count)], target.at[span(rows, count)], send, sem, device)

    loads[0].wait()
    halo = ship(x0, x0, edge(r), 2, 0, halo_sem.at[0], (l, o))
    halo.start()
    halo_in = ship(x0, x0, edge(o), 2, 0, halo_sem.at[0], (l, o))

    inner_here = pl.ds(pl.multiple_of(2 * r * W, W), 6 * W)
    edge_here = pl.ds(pl.multiple_of((6 - 6 * r) * W, W), 2 * W)
    nets = [
        remote(net_input, x1.at[span(own, BAND)], 1, x1_sem.at[0], (l, o)),
        remote(net_input.at[inner_here], x2.at[span(inner(r), 6)], 2, x2_sem.at[r, 0], (l, o)),
        remote(net_input.at[edge_here], x2.at[span(edge(r), 2)], 3, x2_sem.at[r, 1], (l, o)),
    ]
    nets_here = [
        pltpu.make_async_copy(net_input.at[edge_here], x1.at[span(edge(r), 2)], x1_sem.at[1]),
        pltpu.make_async_copy(net_input.at[inner_here], x2.at[span(inner(r), 6)], x2_sem.at[r, 0]),
        pltpu.make_async_copy(net_input.at[edge_here], x2.at[span(edge(r), 2)], x2_sem.at[r, 1]),
    ]
    adj_last = remote(cotangent, adj.at[flat(own, BAND)], 4, adj_sem.at[r], (l, o))
    adj_last_here = pltpu.make_async_copy(cotangent, adj.at[flat(own, BAND)], adj_sem.at[r])
    adj_cross = remote(adj_guess, adj.at[flat(own, BAND)], 5, adj_sem.at[r], (down, o))
    adj_same = remote(adj_guess, adj.at[flat(own, BAND)], 6, adj_sem.at[r], (down, r))

    @pl.when(first)
    def _():
        for copy in nets + nets_here:
            copy.start()

    @pl.when(last)
    def _():
        adj_last.start()
        adj_last_here.start()

    def sweep(src, dst, band, rest, edge_in, send):
        advance(src, mid, weights, 0, 9 * band, 7)
        rest()
        advance(mid, dst, weights, 1, inner(band), 6)
        send(inner(band), 6, 0)
        edge_in.wait_recv()
        advance(src, mid, weights, 0, 7, 2)
        advance(mid, dst, weights, 1, edge(band), 2)
        send(edge(band), 2, 1)

    def send1(rows, count, part):
        @pl.when(passes)
        def _():
            ship(end1, x1, rows, count, 8 + part, x1_sem.at[0], (up, t)).start()
            if part:
                ship(end1, x1, rows, count, 10, x1_sem.at[1], (up, 1 - t)).start()

        if not part:

            @pl.when(even)
            def _():
                ship(end1, x1, rows, count, 17, x1_sem.at[2], (up, 1 - t)).start()

    loads[1].wait()
    sweep(x0, end1, r, loads[2].wait, halo_in, send1)

    @pl.when(takes)
    def _():
        adj_cross.start()

    @pl.when(odd)
    def _():
        adj_same.start()

    def send2(rows, count, part):
        @pl.when(passes)
        def _():
            ship(end2, x2, rows, count, 11 + part, x2_sem.at[s, part], (up, o)).start()

        @pl.when(even)
        def _():
            ship(end2, x2, rows, count, 13 + part, x2_sem.at[s, part], (up, r)).start()

    ship(end1, x1, s * BAND, BAND, 8, x1_sem.at[0], (l, o)).wait_recv()
    x1_edge = ship(end1, x1, edge(1 - s), 2, 10, x1_sem.at[1], (l, o))
    sweep(x1, end2, s, lambda: None, x1_edge, send2)

    adj_in = remote(adj_guess, adj.at[flat(other, BAND)], 5, adj_sem.at[o], (l, o))
    adj_on = remote(adj.at[flat(other, BAND)], adj.at[flat(other, BAND)], 7, adj_sem.at[o], (l, o))

    @pl.when(odd & passes)
    def _():
        ship(end1, x1, inner(1 - s), 6, 17, x1_sem.at[2], (l, o)).wait_recv()
        advance(x1, mid, weights, 0, 9 * (1 - s), 7)
        advance(mid, end2, weights, 1, (1 - s) * BAND, BAND)
        for part, rows, count in ((0, inner(1 - s), 6), (1, edge(1 - s), 2)):
            ship(end2, x2, rows, count, 15 + part, x2_sem.at[1 - s, part], (up, o)).start()
        adj_in.wait_recv()
        adj_on.start()

    @pl.when(odd & last)
    def _():
        ship(end1, x1, inner(1 - s), 6, 17, x1_sem.at[2], (l, o)).wait_recv()

    for part, rows, count in ((0, inner(o), 6), (1, edge(o), 2)):
        ship(end2, x2, rows, count, 11, x2_sem.at[o, part], (l, o)).wait_recv()
    advance(x2, mid3, weights, 0, 9 * o, 7, pre1)

    def second(row, count):
        value = conv(mid3, weights, 1, row, count)
        pre2[flat(row, count), :] = value

    second(inner(o), 6)
    for part, rows, count in ((0, inner(r), 6), (1, edge(r), 2)):
        ship(end2, x2, rows, count, 11, x2_sem.at[r, part], (l, o)).wait_recv()
    outs = [pltpu.make_async_copy(x2.at[span(0, ROWS)], states_out, out_sem.at[0])]
    outs[-1].start()
    advance(x2, mid3, weights, 0, 7 * r, 9, pre1)
    outs.append(pltpu.make_async_copy(mid3.at[span(0, ROWS)], middle_out, out_sem.at[1]))
    outs[-1].start()
    second(6 * r, 10)

    remote(cotangent, adj.at[flat(own, BAND)], 4, adj_sem.at[r], (l, o)).wait_recv()

    @pl.when(even | last)
    def _():
        adj_in.wait_recv()

    delta2[span(0, ROWS), :] = (half_slope(pre2[...]) * adj[...].astype(F32)).astype(BF16)
    half = pl.ds(pl.multiple_of(r * 128, 128), 128)
    outs.append(pltpu.make_async_copy(delta2.at[span(0, ROWS), half], delta2_out, out_sem.at[2]))
    outs[-1].start()

    value = conv(delta2, weights, 1, 0, ROWS, back=True)
    value = (adj[...].astype(F32) + value).astype(BF16)
    back[...] = value
    delta1[span(0, ROWS), :] = (half_slope(pre1[...]) * value.astype(F32)).astype(BF16)
    outs.append(pltpu.make_async_copy(delta1.at[span(0, ROWS), half], delta1_out, out_sem.at[3]))
    outs[-1].start()

    value = conv(delta1, weights, 0, own, BAND, back=True)
    adj_own[...] = (back[flat(own, BAND), :].astype(F32) + value).astype(BF16)
    outs.append(pltpu.make_async_copy(adj_own, adjoint_out, out_sem.at[4]))
    outs[-1].start()

    halo.wait_send()

    @pl.when(first)
    def _():
        for copy in nets:
            copy.wait_send()

    @pl.when(last)
    def _():
        adj_last.wait_send()

    @pl.when(takes)
    def _():
        adj_cross.wait_send()

    @pl.when(odd)
    def _():
        adj_same.wait_send()

    @pl.when(odd & passes)
    def _():
        adj_on.wait_send()

    @pl.when(passes)
    def _():
        for rows, count, send in ((inner(r), 6, 8), (edge(r), 2, 9), (edge(r), 2, 10)):
            ship(end1, x1, rows, count, send, x1_sem.at[0], (l, o)).wait_send()
        for rows, count, send in ((inner(s), 6, 11), (edge(s), 2, 12)):
            ship(end2, x2, rows, count, send, x2_sem.at[0, 0], (l, o)).wait_send()

    @pl.when(even)
    def _():
        ship(end1, x1, inner(r), 6, 17, x1_sem.at[2], (l, o)).wait_send()
        for rows, count, send in ((inner(s), 6, 13), (edge(s), 2, 14)):
            ship(end2, x2, rows, count, send, x2_sem.at[0, 0], (l, o)).wait_send()

    @pl.when(odd & passes)
    def _():
        for rows, count, send in ((inner(1 - s), 6, 15), (edge(1 - s), 2, 16)):
            ship(end2, x2, rows, count, send, x2_sem.at[0, 0], (l, o)).wait_send()

    for copy in outs:
        copy.wait()


def grad_kernel(
    scale,
    states, middle, delta1, delta2, adjoint,
    states_out, adjoint_out, grad_out,
    x, m, d1, d2, adj, wide, grads, sem, out_sem,
):
    r = lax.axis_index("rows")
    loads = [
        pltpu.make_async_copy(middle, m, sem.at[0]),
        pltpu.make_async_copy(delta2, d2, sem.at[1]),
        pltpu.make_async_copy(states, x, sem.at[2]),
        pltpu.make_async_copy(delta1, d1, sem.at[3]),
        pltpu.make_async_copy(adjoint, adj, sem.at[4]),
    ]
    for copy in loads:
        copy.start()
    outs = []
    zero = jnp.zeros((W, 384), BF16)
    for layer in range(2):
        wide[layer, pl.ds(0, W), :] = zero
        wide[layer, pl.ds((ROWS + 1) * W, W), :] = zero
    col = lax.broadcasted_iota(jnp.int32, (PX, 128), 0) % W
    for layer, image, delta, pair in ((1, m, d2, 0), (0, x, d1, 2)):
        loads[pair].wait()
        loads[pair + 1].wait()
        if layer == 0:
            loads[4].wait()
            outs.append(pltpu.make_async_copy(x.at[flat(r * BAND, BAND)], states_out, out_sem.at[0]))
            outs.append(pltpu.make_async_copy(adj, adjoint_out, out_sem.at[1]))
            for copy in outs[-2:]:
                copy.start()
        value = delta[...].astype(F32)
        after = jnp.where(col == W - 1, 0.0, pltpu.roll(value, PX - 1, 0))
        before = jnp.where(col == 0, 0.0, pltpu.roll(value, 1, 0))
        wide[layer, pl.ds(W, PX), 0:128] = after.astype(BF16)
        wide[layer, pl.ds(W, PX), 128:256] = delta[...]
        wide[layer, pl.ds(W, PX), 256:384] = before.astype(BF16)
        side = jnp.concatenate([wide[layer, pl.ds((2 - a) * W, PX), :] for a in range(3)], axis=1)
        terms = lax.dot_general(
            image[...], side, (((0,), (0,)), ((), ())), preferred_element_type=F32
        )
        for tap in range(9):
            grads[layer, tap] = terms[:, tap * 128 : (tap + 1) * 128] * scale
        outs.append(pltpu.make_async_copy(grads.at[layer], grad_out.at[layer], out_sem.at[2 + layer]))
        outs[-1].start()
    for copy in outs:
        copy.wait()


def solution(mesh):
    layers = mesh.shape["layer"]
    scale = 1.0 / math.sqrt(PX)
    hbm = pl.BlockSpec(memory_space=pl.ANY)
    image = lambda rows: pltpu.VMEM((rows * W, C), BF16)

    def local(guess, adj_guess, weights, net_input, cotangent):
        args = (
            guess.reshape(BPX, C),
            adj_guess.reshape(BPX, C),
            weights.reshape(18, C, C),
            net_input.reshape(BPX, C),
            cotangent.reshape(BPX, C),
        )
        sds = jax.ShapeDtypeStruct
        states, middle, delta1, delta2, adjoint = pl.pallas_call(
            lambda *refs: sweep_kernel(layers, *refs),
            out_shape=(
                sds((PX, C), BF16), sds((PX, C), BF16), sds((PX, 128), BF16), sds((PX, 128), BF16),
                sds((BPX, C), BF16),
            ),
            in_specs=[hbm] * 5,
            out_specs=[hbm] * 5,
            scratch_shapes=[
                pltpu.VMEM((18, C, C), BF16),
                image(18), image(18), image(18), image(18), image(18), image(18), image(18),
                image(16), image(18), image(16), image(18),
                pltpu.VMEM((PX, C), F32),
                pltpu.VMEM((PX, C), F32),
                image(8),
                pltpu.SemaphoreType.DMA((3,)),
                pltpu.SemaphoreType.DMA((18,)),
                pltpu.SemaphoreType.DMA((1,)),
                pltpu.SemaphoreType.DMA((3,)),
                pltpu.SemaphoreType.DMA((2, 2)),
                pltpu.SemaphoreType.DMA((2,)),
                pltpu.SemaphoreType.DMA((5,)),
            ],
            compiler_params=pltpu.CompilerParams(
                collective_id=0, has_side_effects=True, vmem_limit_bytes=60 << 20
            ),
            name="sweeps",
        )(*args)
        states, adjoint, grads = pl.pallas_call(
            lambda *refs: grad_kernel(scale, *refs),
            out_shape=(sds((BPX, C), BF16), sds((BPX, C), BF16), sds((2, 9, C, 128), F32)),
            in_specs=[hbm] * 5,
            out_specs=[hbm] * 3,
            scratch_shapes=[
                image(16), image(16),
                pltpu.VMEM((PX, 128), BF16), pltpu.VMEM((PX, 128), BF16),
                image(8),
                pltpu.VMEM((2, 18 * W, 384), BF16),
                pltpu.VMEM((2, 9, C, 128), F32),
                pltpu.SemaphoreType.DMA((5,)),
                pltpu.SemaphoreType.DMA((4,)),
            ],
            compiler_params=pltpu.CompilerParams(vmem_limit_bytes=56 << 20),
            name="weight_grads",
        )(states, middle, delta1, delta2, adjoint)
        shape = (1, 1, BAND, W, C)
        return states.reshape(shape), adjoint.reshape(shape), grads

    in_specs = (
        P("layer", None, "rows", None, None),
        P("layer", None, "rows", None, None),
        P("layer", None, None, None),
        P(None, "rows", None, None),
        P(None, "rows", None, None),
    )
    out_specs = (
        P("layer", None, "rows", None, None),
        P("layer", None, "rows", None, None),
        P("layer", None, None, "rows"),
    )
    return jax.shard_map(local, mesh=mesh, in_specs=in_specs, out_specs=out_specs, check_vma=False)
```

```python
import math

import jax
import jax.numpy as jnp
from jax import lax
from jax.experimental import pallas as pl
from jax.experimental.pallas import tpu as pltpu
from jax.sharding import PartitionSpec as P

MESH = pl.DeviceIdType.MESH
F32 = jnp.float32
BF16 = jnp.bfloat16
ROWS = 16
BAND = 8
W = 64
C = 256
PX = ROWS * W
BPX = BAND * W


def span(row, count):
    start = (row + 1) * W
    return pl.ds(start if isinstance(start, int) else pl.multiple_of(start, W), count * W)


def flat(row, count):
    start = row * W
    return pl.ds(start if isinstance(start, int) else pl.multiple_of(start, W), count * W)


def conv(src, weights, layer, row, count, back=False):
    n = count * W
    shifted = []
    for b in range(3):
        acc = None
        for a in range(3):
            window = src[span(row + a - 1, count), :]
            if back:
                term = lax.dot_general(
                    window,
                    weights[layer * 9 + (2 - a) * 3 + (2 - b)],
                    (((1,), (1,)), ((), ())),
                    preferred_element_type=F32,
                )
            else:
                term = jnp.dot(window, weights[layer * 9 + a * 3 + b], preferred_element_type=F32)
            acc = term if acc is None else acc + term
        shifted.append(acc)
    col = lax.broadcasted_iota(jnp.int32, (n, C), 0) % W
    left = jnp.where(col == 0, 0.0, pltpu.roll(shifted[0], 1, 0))
    right = jnp.where(col == W - 1, 0.0, pltpu.roll(shifted[2], n - 1, 0))
    return shifted[1] + left + right


def advance(src, dst, weights, layer, row, count, pre=None):
    value = conv(src, weights, layer, row, count)
    state = src[span(row, count), :].astype(F32)
    dst[span(row, count), :] = (state + 0.5 * value / (1.0 + jnp.exp(-value))).astype(BF16)
    if pre is not None:
        pre[flat(row, count), :] = value


def half_slope(value):
    s = 1.0 / (1.0 + jnp.exp(-value))
    return 0.5 * s * (1.0 + value * (1.0 - s))


def sweep_kernel(
    layers,
    guess, adj_guess, weights_hbm, net_input, cotangent,
    states_out, middle_out, delta1_out, delta2_out, adjoint_out,
    weights, x0, x1, x2, mid, mid3, end1, end2, adj, delta2, back, delta1, pre1, pre2, adj_own,
    load_sem, send_sem, halo_sem, x1_sem, x2_sem, adj_sem, out_sem,
):
    l = lax.axis_index("layer")
    r = lax.axis_index("rows")
    o = 1 - r
    even = l % 2 == 0
    odd = l % 2 == 1
    first = l == 0
    last = l == layers - 1
    passes = jnp.logical_not(last)
    takes = jnp.logical_not(first)
    up = jnp.minimum(l + 1, layers - 1)
    down = jnp.maximum(l - 1, 0)
    t = (r + l) % 2
    s = jnp.where(first, r, (r + l + 1) % 2)
    own = r * BAND
    other = o * BAND

    loads = [
        pltpu.make_async_copy(guess, x0.at[span(own, BAND)], load_sem.at[0]),
        pltpu.make_async_copy(weights_hbm.at[pl.ds(0, 9)], weights.at[pl.ds(0, 9)], load_sem.at[1]),
        pltpu.make_async_copy(weights_hbm.at[pl.ds(9, 9)], weights.at[pl.ds(9, 9)], load_sem.at[2]),
    ]
    for copy in loads:
        copy.start()

    barrier = pltpu.get_barrier_semaphore()
    pl.semaphore_signal(barrier, inc=1, device_id=(l, o), device_id_type=MESH)

    @pl.when(jnp.logical_not(first))
    def _():
        pl.semaphore_signal(barrier, inc=1, device_id=(down, r), device_id_type=MESH)
        pl.semaphore_signal(barrier, inc=1, device_id=(down, o), device_id_type=MESH)

    @pl.when(jnp.logical_not(last))
    def _():
        pl.semaphore_signal(barrier, inc=1, device_id=(up, r), device_id_type=MESH)
        pl.semaphore_signal(barrier, inc=1, device_id=(up, o), device_id_type=MESH)

    zero = jnp.zeros((W, C), BF16)
    for buf in (x0, x1, x2, mid, mid3, delta2, delta1):
        buf[pl.ds(0, W), :] = zero
        buf[pl.ds((ROWS + 1) * W, W), :] = zero

    @pl.when(first | last)
    def _():
        pl.semaphore_wait(barrier, 3)

    @pl.when(jnp.logical_not(first | last))
    def _():
        pl.semaphore_wait(barrier, 5)

    def remote(src, dst, send, recv, device):
        return pltpu.make_async_remote_copy(
            src_ref=src, dst_ref=dst, send_sem=send_sem.at[send], recv_sem=recv,
            device_id=device, device_id_type=MESH,
        )

    edge = lambda band: 6 + 2 * band
    near = lambda band: 4 + 6 * band
    far = lambda band: 12 * band
    inner = lambda band: 10 * band
    parts = ((far, 4), (near, 2), (edge, 2))

    def ship(buf, target, rows, count, send, sem, device):
        return remote(buf.at[span(rows, count)], target.at[span(rows, count)], send, sem, device)

    loads[0].wait()
    halo = ship(x0, x0, edge(r), 2, 0, halo_sem.at[0], (l, o))
    halo.start()
    halo_in = ship(x0, x0, edge(o), 2, 0, halo_sem.at[0], (l, o))

    net_at = lambda rows, count: net_input.at[flat(rows - own, count)]
    net1 = remote(net_at(edge(r), 2), x1.at[span(edge(r), 2)], 1, x1_sem.at[1], (l, o))
    nets2 = [
        remote(net_at(rows(r), count), x2.at[span(rows(r), count)], 2 + part, x2_sem.at[r, part], (l, o))
        for part, (rows, count) in enumerate(parts)
    ]
    nets_here = [pltpu.make_async_copy(net_input, x1.at[span(own, BAND)], x1_sem.at[0])] + [
        pltpu.make_async_copy(net_at(rows(r), count), x2.at[span(rows(r), count)], x2_sem.at[r, part])
        for part, (rows, count) in enumerate(parts)
    ]
    adj_last = remote(cotangent, adj.at[flat(own, BAND)], 5, adj_sem.at[r], (l, o))
    adj_last_here = pltpu.make_async_copy(cotangent, adj.at[flat(own, BAND)], adj_sem.at[r])
    adj_cross = remote(adj_guess, adj.at[flat(own, BAND)], 6, adj_sem.at[r], (down, o))
    adj_same = remote(adj_guess, adj.at[flat(own, BAND)], 7, adj_sem.at[r], (down, r))

    @pl.when(first)
    def _():
        net1.start()
        for copy in nets_here:
            copy.start()

    @pl.when(takes)
    def _():
        adj_cross.start()

    @pl.when(odd)
    def _():
        adj_same.start()

    def sweep(src, dst, band, rest, edge_in, send):
        advance(src, mid, weights, 0, 9 * band, 7)
        rest()
        advance(mid, dst, weights, 1, inner(band), 6)
        send(False)
        edge_in.wait_recv()
        advance(src, mid, weights, 0, 7, 2)
        advance(mid, dst, weights, 1, edge(band), 2)
        send(True)

    e1_inner = ship(end1, x1, inner(r), 6, 9, x1_sem.at[0], (up, t))
    e1_edge = ship(end1, x1, edge(r), 2, 10, x1_sem.at[0], (up, t))
    e1_cross = ship(end1, x1, edge(r), 2, 11, x1_sem.at[1], (up, 1 - t))
    e1_rest = ship(end1, x1, inner(r), 6, 12, x1_sem.at[2], (up, o))

    def send1(late):
        @pl.when(passes)
        def _():
            if late:
                e1_cross.start()
                e1_edge.start()
            else:
                e1_inner.start()

        if late:

            @pl.when(even)
            def _():
                e1_rest.start()

    loads[1].wait()
    sweep(x0, end1, r, loads[2].wait, halo_in, send1)

    @pl.when(first)
    def _():
        for copy in nets2[::-1]:
            copy.start()

    @pl.when(last)
    def _():
        adj_last.start()
        adj_last_here.start()

    adj_in = remote(adj_guess, adj.at[flat(other, BAND)], 6, adj_sem.at[o], (l, o))
    adj_on = remote(adj.at[flat(other, BAND)], adj.at[flat(other, BAND)], 8, adj_sem.at[o], (l, o))

    e2 = [
        ship(end2, x2, rows(s), count, 13 + part, x2_sem.at[s, part], (up, o))
        for part, (rows, count) in enumerate(parts)
    ]
    e2_same = [
        ship(end2, x2, rows(s), count, 16 + part, x2_sem.at[s, part], (up, r))
        for part, (rows, count) in enumerate(parts)
    ]

    def send2(late):
        which = slice(2, 3) if late else slice(0, 2)

        @pl.when(passes)
        def _():
            for copy in e2[which]:
                copy.start()

    q = 1 - s
    x1_own = ship(end1, x1, s * BAND, BAND, 9, x1_sem.at[0], (l, o))
    x1_edge = ship(end1, x1, edge(q), 2, 11, x1_sem.at[1], (l, o))
    x1_rest = ship(end1, x1, inner(q), 6, 12, x1_sem.at[2], (l, o))
    e2_other = [
        ship(end2, x2, rows(q), count, 19 + part, x2_sem.at[q, part], (up, o))
        for part, (rows, count) in enumerate(parts)
    ]

    distant = l % 16 == 15

    def pass_adjoint(here):
        @pl.when(here & passes)
        def _():
            adj_in.wait_recv()
            adj_on.start()

    @pl.when(even)
    def _():
        x1_own.wait_recv()
        x1_edge.wait_recv()
        advance(x1, mid, weights, 0, 7 * s, 9)
        advance(mid, end2, weights, 1, s * BAND, BAND)
        for part in (2, 1, 0):
            e2_same[part].start()
            e2[part].start()

    @pl.when(odd)
    def _():
        x1_own.wait_recv()
        sweep(x1, end2, s, lambda: None, x1_edge, send2)
        pass_adjoint(jnp.logical_not(distant))
        x1_rest.wait_recv()

        @pl.when(passes)
        def _():
            advance(x1, mid, weights, 0, 3 + 6 * q, 4)
            advance(mid, end2, weights, 1, 4 + 4 * q, 4)
            for copy in e2_other[1:]:
                copy.start()
            advance(x1, mid, weights, 0, 13 * q, 3)
            advance(mid, end2, weights, 1, far(q), 4)
            e2_other[0].start()

        pass_adjoint(distant)

    x2_in = lambda band, part: ship(
        end2, x2, parts[part][0](band), parts[part][1], 13, x2_sem.at[band, part], (l, o)
    ).wait_recv()
    f = jnp.where(l < 2, r, o)
    g = 1 - f
    for part in range(3):
        x2_in(f, part)
    advance(x2, mid3, weights, 0, 9 * f, 7, pre1)

    def second(row, count):
        pre2[flat(row, count), :] = conv(mid3, weights, 1, row, count)

    def turn(row, count):
        value = half_slope(pre2[flat(row, count), :]) * adj[flat(row, count), :].astype(F32)
        delta2[span(row, count), :] = value.astype(BF16)

    def turn_back(row, count):
        value = conv(delta2, weights, 1, row, count, back=True)
        value = (adj[flat(row, count), :].astype(F32) + value).astype(BF16)
        back[flat(row, count), :] = value
        value = half_slope(pre1[flat(row, count), :]) * value.astype(F32)
        delta1[span(row, count), :] = value.astype(BF16)

    second(inner(f), 6)
    x2_in(g, 1)
    x2_in(g, 2)
    advance(x2, mid3, weights, 0, 7 - 2 * f, 4, pre1)
    second(6, 4)
    remote(cotangent, adj.at[flat(own, BAND)], 5, adj_sem.at[r], (l, o)).wait_recv()

    @pl.when(even | last)
    def _():
        adj_in.wait_recv()

    turn(6 * f, 10)
    turn_back(7 * f, 9)

    x2_in(g, 0)
    half = pl.ds(pl.multiple_of(r * 128, 128), 128)
    outs = [pltpu.make_async_copy(x2.at[span(0, ROWS)], states_out, out_sem.at[0])]
    outs[-1].start()
    advance(x2, mid3, weights, 0, 11 * g, 5, pre1)
    outs.append(pltpu.make_async_copy(mid3.at[span(0, ROWS)], middle_out, out_sem.at[1]))
    outs[-1].start()
    second(10 * g, 6)
    turn(10 * g, 6)
    outs.append(pltpu.make_async_copy(delta2.at[span(0, ROWS), half], delta2_out, out_sem.at[2]))
    outs[-1].start()
    turn_back(9 * g, 7)
    outs.append(pltpu.make_async_copy(delta1.at[span(0, ROWS), half], delta1_out, out_sem.at[3]))
    outs[-1].start()

    value = conv(delta1, weights, 0, own, BAND, back=True)
    adj_own[...] = (back[flat(own, BAND), :].astype(F32) + value).astype(BF16)
    outs.append(pltpu.make_async_copy(adj_own, adjoint_out, out_sem.at[4]))
    outs[-1].start()

    halo.wait_send()
    for here, copies in (
        (first, [net1] + nets2),
        (last, [adj_last]),
        (takes, [adj_cross]),
        (odd, [adj_same]),
        (odd & passes, [adj_on] + e2_other),
        (passes, [e1_inner, e1_edge, e1_cross] + e2),
        (even, [e1_rest] + e2_same),
    ):

        @pl.when(here)
        def _(copies=copies):
            for copy in copies:
                copy.wait_send()

    for copy in outs:
        copy.wait()


def grad_kernel(
    scale,
    states, middle, delta1, delta2, adjoint,
    states_out, adjoint_out, grad_out,
    x, m, d1, d2, adj, wide, grads, sem, out_sem,
):
    r = lax.axis_index("rows")
    loads = [
        pltpu.make_async_copy(middle, m, sem.at[0]),
        pltpu.make_async_copy(delta2, d2, sem.at[1]),
        pltpu.make_async_copy(states, x, sem.at[2]),
        pltpu.make_async_copy(delta1, d1, sem.at[3]),
        pltpu.make_async_copy(adjoint, adj, sem.at[4]),
    ]
    for copy in loads:
        copy.start()
    outs = []
    zero = jnp.zeros((W, 384), BF16)
    for layer in range(2):
        wide[layer, pl.ds(0, W), :] = zero
        wide[layer, pl.ds((ROWS + 1) * W, W), :] = zero
    col = lax.broadcasted_iota(jnp.int32, (PX, 128), 0) % W
    for layer, image, delta, pair in ((1, m, d2, 0), (0, x, d1, 2)):
        loads[pair].wait()
        loads[pair + 1].wait()
        if layer == 0:
            loads[4].wait()
            outs.append(pltpu.make_async_copy(x.at[flat(r * BAND, BAND)], states_out, out_sem.at[0]))
            outs.append(pltpu.make_async_copy(adj, adjoint_out, out_sem.at[1]))
            for copy in outs[-2:]:
                copy.start()
        value = delta[...].astype(F32)
        after = jnp.where(col == W - 1, 0.0, pltpu.roll(value, PX - 1, 0))
        before = jnp.where(col == 0, 0.0, pltpu.roll(value, 1, 0))
        wide[layer, pl.ds(W, PX), 0:128] = after.astype(BF16)
        wide[layer, pl.ds(W, PX), 128:256] = delta[...]
        wide[layer, pl.ds(W, PX), 256:384] = before.astype(BF16)
        side = jnp.concatenate([wide[layer, pl.ds((2 - a) * W, PX), :] for a in range(3)], axis=1)
        terms = lax.dot_general(
            image[...], side, (((0,), (0,)), ((), ())), preferred_element_type=F32
        )
        for tap in range(9):
            grads[layer, tap] = terms[:, tap * 128 : (tap + 1) * 128] * scale
        outs.append(pltpu.make_async_copy(grads.at[layer], grad_out.at[layer], out_sem.at[2 + layer]))
        outs[-1].start()
    for copy in outs:
        copy.wait()


def solution(mesh):
    layers = mesh.shape["layer"]
    scale = 1.0 / math.sqrt(PX)
    hbm = pl.BlockSpec(memory_space=pl.ANY)
    image = lambda rows: pltpu.VMEM((rows * W, C), BF16)

    def local(guess, adj_guess, weights, net_input, cotangent):
        args = (
            guess.reshape(BPX, C),
            adj_guess.reshape(BPX, C),
            weights.reshape(18, C, C),
            net_input.reshape(BPX, C),
            cotangent.reshape(BPX, C),
        )
        sds = jax.ShapeDtypeStruct
        states, middle, delta1, delta2, adjoint = pl.pallas_call(
            lambda *refs: sweep_kernel(layers, *refs),
            out_shape=(
                sds((PX, C), BF16), sds((PX, C), BF16), sds((PX, 128), BF16), sds((PX, 128), BF16),
                sds((BPX, C), BF16),
            ),
            in_specs=[hbm] * 5,
            out_specs=[hbm] * 5,
            scratch_shapes=[
                pltpu.VMEM((18, C, C), BF16),
                image(18), image(18), image(18), image(18), image(18), image(18), image(18),
                image(16), image(18), image(16), image(18),
                pltpu.VMEM((PX, C), F32),
                pltpu.VMEM((PX, C), F32),
                image(8),
                pltpu.SemaphoreType.DMA((3,)),
                pltpu.SemaphoreType.DMA((22,)),
                pltpu.SemaphoreType.DMA((1,)),
                pltpu.SemaphoreType.DMA((3,)),
                pltpu.SemaphoreType.DMA((2, 3)),
                pltpu.SemaphoreType.DMA((2,)),
                pltpu.SemaphoreType.DMA((5,)),
            ],
            compiler_params=pltpu.CompilerParams(
                collective_id=0, has_side_effects=True, vmem_limit_bytes=60 << 20
            ),
            name="sweeps",
        )(*args)
        states, adjoint, grads = pl.pallas_call(
            lambda *refs: grad_kernel(scale, *refs),
            out_shape=(sds((BPX, C), BF16), sds((BPX, C), BF16), sds((2, 9, C, 128), F32)),
            in_specs=[hbm] * 5,
            out_specs=[hbm] * 3,
            scratch_shapes=[
                image(16), image(16),
                pltpu.VMEM((PX, 128), BF16), pltpu.VMEM((PX, 128), BF16),
                image(8),
                pltpu.VMEM((2, 18 * W, 384), BF16),
                pltpu.VMEM((2, 9, C, 128), F32),
                pltpu.SemaphoreType.DMA((5,)),
                pltpu.SemaphoreType.DMA((4,)),
            ],
            compiler_params=pltpu.CompilerParams(vmem_limit_bytes=56 << 20),
            name="weight_grads",
        )(states, middle, delta1, delta2, adjoint)
        shape = (1, 1, BAND, W, C)
        return states.reshape(shape), adjoint.reshape(shape), grads

    in_specs = (
        P("layer", None, "rows", None, None),
        P("layer", None, "rows", None, None),
        P("layer", None, None, None),
        P(None, "rows", None, None),
        P(None, "rows", None, None),
    )
    out_specs = (
        P("layer", None, "rows", None, None),
        P("layer", None, "rows", None, None),
        P("layer", None, None, "rows"),
    )
    return jax.shard_map(local, mesh=mesh, in_specs=in_specs, out_specs=out_specs, check_vma=False)
```

```python
import math

import jax
import jax.numpy as jnp
from jax import lax
from jax.experimental import pallas as pl
from jax.experimental.pallas import tpu as pltpu
from jax.sharding import PartitionSpec as P

MESH = pl.DeviceIdType.MESH
F32 = jnp.float32
BF16 = jnp.bfloat16
ROWS = 16
BAND = 8
W = 64
C = 256
PX = ROWS * W
BPX = BAND * W


def span(row, count):
    start = (row + 1) * W
    return pl.ds(start if isinstance(start, int) else pl.multiple_of(start, W), count * W)


def flat(row, count):
    start = row * W
    return pl.ds(start if isinstance(start, int) else pl.multiple_of(start, W), count * W)


def conv(src, weights, layer, row, count, back=False):
    n = count * W
    shifted = []
    for b in range(3):
        acc = None
        for a in range(3):
            window = src[span(row + a - 1, count), :]
            if back:
                term = lax.dot_general(
                    window,
                    weights[layer * 9 + (2 - a) * 3 + (2 - b)],
                    (((1,), (1,)), ((), ())),
                    preferred_element_type=F32,
                )
            else:
                term = jnp.dot(window, weights[layer * 9 + a * 3 + b], preferred_element_type=F32)
            acc = term if acc is None else acc + term
        shifted.append(acc)
    col = lax.broadcasted_iota(jnp.int32, (n, C), 0) % W
    left = jnp.where(col == 0, 0.0, pltpu.roll(shifted[0], 1, 0))
    right = jnp.where(col == W - 1, 0.0, pltpu.roll(shifted[2], n - 1, 0))
    return shifted[1] + left + right


def sigmoid(value):
    return 1.0 / (1.0 + jnp.exp(-value))


def half_slope(value, s):
    return 0.5 * s * (1.0 + value * (1.0 - s))


def advance(src, dst, weights, layer, row, count, slope=None):
    value = conv(src, weights, layer, row, count)
    s = sigmoid(value)
    state = src[span(row, count), :].astype(F32)
    dst[span(row, count), :] = (state + 0.5 * value * s).astype(BF16)
    if slope is not None:
        slope[flat(row, count), :] = half_slope(value, s)


def sweep_kernel(
    layers,
    guess, adj_guess, weights_hbm, net_input, cotangent,
    states_out, middle_out, delta1_out, delta2_out, adjoint_out,
    weights, x0, x1, x2, mid, mid3, end1, end2, adj, delta2, back, delta1, slope1, slope2,
    load_sem, send_sem, halo_sem, x1_sem, x2_sem, adj_sem, out_sem,
):
    l = lax.axis_index("layer")
    r = lax.axis_index("rows")
    o = 1 - r
    even = l % 2 == 0
    odd = l % 2 == 1
    first = l == 0
    last = l == layers - 1
    passes = jnp.logical_not(last)
    takes = jnp.logical_not(first)
    up = jnp.minimum(l + 1, layers - 1)
    down = jnp.maximum(l - 1, 0)
    t = (r + l) % 2
    s = jnp.where(first, r, (r + l + 1) % 2)
    own = r * BAND
    other = o * BAND

    loads = [
        pltpu.make_async_copy(guess, x0.at[span(own, BAND)], load_sem.at[0]),
        pltpu.make_async_copy(weights_hbm.at[pl.ds(0, 9)], weights.at[pl.ds(0, 9)], load_sem.at[1]),
        pltpu.make_async_copy(weights_hbm.at[pl.ds(9, 9)], weights.at[pl.ds(9, 9)], load_sem.at[2]),
    ]
    for copy in loads:
        copy.start()

    barrier = pltpu.get_barrier_semaphore()
    pl.semaphore_signal(barrier, inc=1, device_id=(l, o), device_id_type=MESH)

    @pl.when(jnp.logical_not(first))
    def _():
        pl.semaphore_signal(barrier, inc=1, device_id=(down, r), device_id_type=MESH)
        pl.semaphore_signal(barrier, inc=1, device_id=(down, o), device_id_type=MESH)

    @pl.when(jnp.logical_not(last))
    def _():
        pl.semaphore_signal(barrier, inc=1, device_id=(up, r), device_id_type=MESH)
        pl.semaphore_signal(barrier, inc=1, device_id=(up, o), device_id_type=MESH)

    zero = jnp.zeros((W, C), BF16)
    for buf in (x0, x1, x2, mid, mid3, delta2, delta1):
        buf[pl.ds(0, W), :] = zero
        buf[pl.ds((ROWS + 1) * W, W), :] = zero

    @pl.when(first | last)
    def _():
        pl.semaphore_wait(barrier, 3)

    @pl.when(jnp.logical_not(first | last))
    def _():
        pl.semaphore_wait(barrier, 5)

    def remote(src, dst, send, recv, device):
        return pltpu.make_async_remote_copy(
            src_ref=src, dst_ref=dst, send_sem=send_sem.at[send], recv_sem=recv,
            device_id=device, device_id_type=MESH,
        )

    edge = lambda band: 6 + 2 * band
    near = lambda band: 4 + 6 * band
    far = lambda band: 12 * band
    inner = lambda band: 10 * band
    parts = ((far, 4), (near, 2), (edge, 2))

    def ship(buf, target, rows, count, send, sem, device):
        return remote(buf.at[span(rows, count)], target.at[span(rows, count)], send, sem, device)

    loads[0].wait()
    halo = ship(x0, x0, edge(r), 2, 0, halo_sem.at[0], (l, o))
    halo.start()
    halo_in = ship(x0, x0, edge(o), 2, 0, halo_sem.at[0], (l, o))

    net_at = lambda rows, count: net_input.at[flat(rows - own, count)]
    net1 = remote(net_at(edge(r), 2), x1.at[span(edge(r), 2)], 1, x1_sem.at[1], (l, o))
    nets2 = [
        remote(net_at(rows(r), count), x2.at[span(rows(r), count)], 2 + part, x2_sem.at[r, part], (l, o))
        for part, (rows, count) in enumerate(parts)
    ]
    nets_here = [pltpu.make_async_copy(net_input, x1.at[span(own, BAND)], x1_sem.at[0])] + [
        pltpu.make_async_copy(net_at(rows(r), count), x2.at[span(rows(r), count)], x2_sem.at[r, part])
        for part, (rows, count) in enumerate(parts)
    ]
    adj_last = remote(cotangent, adj.at[flat(own, BAND)], 5, adj_sem.at[r], (l, o))
    adj_last_here = pltpu.make_async_copy(cotangent, adj.at[flat(own, BAND)], adj_sem.at[r])
    adj_cross = remote(adj_guess, adj.at[flat(own, BAND)], 6, adj_sem.at[r], (down, o))
    adj_same = remote(adj_guess, adj.at[flat(own, BAND)], 7, adj_sem.at[r], (down, r))

    @pl.when(first)
    def _():
        net1.start()
        for copy in nets_here:
            copy.start()

    @pl.when(takes)
    def _():
        adj_cross.start()

    @pl.when(odd)
    def _():
        adj_same.start()

    def sweep(src, dst, band, rest, edge_in, send):
        advance(src, mid, weights, 0, 9 * band, 7)
        rest()
        advance(mid, dst, weights, 1, inner(band), 6)
        send(False)
        edge_in.wait_recv()
        advance(src, mid, weights, 0, 7, 2)
        advance(mid, dst, weights, 1, edge(band), 2)
        send(True)

    e1_inner = ship(end1, x1, inner(r), 6, 9, x1_sem.at[0], (up, t))
    e1_edge = ship(end1, x1, edge(r), 2, 10, x1_sem.at[0], (up, t))
    e1_cross = ship(end1, x1, edge(r), 2, 11, x1_sem.at[1], (up, 1 - t))
    e1_rest = ship(end1, x1, inner(r), 6, 12, x1_sem.at[2], (up, o))

    def send1(late):
        @pl.when(passes)
        def _():
            if late:
                e1_cross.start()
                e1_edge.start()
            else:
                e1_inner.start()

        if late:

            @pl.when(even)
            def _():
                e1_rest.start()

    loads[1].wait()
    sweep(x0, end1, r, loads[2].wait, halo_in, send1)

    @pl.when(last)
    def _():
        adj_last.start()
        adj_last_here.start()

    adj_in = remote(adj_guess, adj.at[flat(other, BAND)], 6, adj_sem.at[o], (l, o))
    adj_on = remote(adj.at[flat(other, BAND)], adj.at[flat(other, BAND)], 8, adj_sem.at[o], (l, o))

    e2 = [
        ship(end2, x2, rows(s), count, 13 + part, x2_sem.at[s, part], (up, o))
        for part, (rows, count) in enumerate(parts)
    ]
    e2_same = [
        ship(end2, x2, rows(s), count, 16 + part, x2_sem.at[s, part], (up, r))
        for part, (rows, count) in enumerate(parts)
    ]

    def send2(late):
        which = slice(2, 3) if late else slice(0, 2)

        @pl.when(passes)
        def _():
            for copy in e2[which]:
                copy.start()

    q = 1 - s
    x1_own = ship(end1, x1, s * BAND, BAND, 9, x1_sem.at[0], (l, o))
    x1_edge = ship(end1, x1, edge(q), 2, 11, x1_sem.at[1], (l, o))
    x1_rest = ship(end1, x1, inner(q), 6, 12, x1_sem.at[2], (l, o))
    e2_other = [
        ship(end2, x2, rows(q), count, 19 + part, x2_sem.at[q, part], (up, o))
        for part, (rows, count) in enumerate(parts)
    ]

    distant = l % 16 == 15

    def pass_adjoint(here):
        @pl.when(here & passes)
        def _():
            adj_in.wait_recv()
            adj_on.start()

    @pl.when(even)
    def _():
        x1_own.wait_recv()
        x1_edge.wait_recv()
        advance(x1, mid, weights, 0, 7 * s, 9)
        advance(mid, end2, weights, 1, s * BAND, BAND)
        for part in (2, 1, 0):
            e2_same[part].start()
            e2[part].start()

        @pl.when(first)
        def _():
            for copy in nets2[::-1]:
                copy.start()

    @pl.when(odd)
    def _():
        x1_own.wait_recv()
        sweep(x1, end2, s, lambda: None, x1_edge, send2)
        pass_adjoint(jnp.logical_not(distant))
        x1_rest.wait_recv()

        @pl.when(passes)
        def _():
            advance(x1, mid, weights, 0, 3 + 6 * q, 4)
            advance(mid, end2, weights, 1, 4 + 4 * q, 4)
            for copy in e2_other[1:]:
                copy.start()
            advance(x1, mid, weights, 0, 13 * q, 3)
            advance(mid, end2, weights, 1, far(q), 4)
            e2_other[0].start()

        pass_adjoint(distant)

    x2_in = lambda band, part: ship(
        end2, x2, parts[part][0](band), parts[part][1], 13, x2_sem.at[band, part], (l, o)
    ).wait_recv()
    f = jnp.where(l < 2, r, o)
    g = 1 - f
    for part in range(3):
        x2_in(f, part)
    advance(x2, mid3, weights, 0, 9 * f, 7, slope1)

    def second(row, count):
        value = conv(mid3, weights, 1, row, count)
        return half_slope(value, sigmoid(value))

    def turn(row, count, slope):
        value = (slope * adj[flat(row, count), :].astype(F32)).astype(BF16)
        delta2[span(row, count), :] = value
        delta2_out[flat(row, count), :] = jnp.where(r == 0, value[:, :128], value[:, 128:])

    def turn_back(row, count):
        value = conv(delta2, weights, 1, row, count, back=True)
        value = (adj[flat(row, count), :].astype(F32) + value).astype(BF16)
        back[flat(row, count), :] = value
        value = slope1[flat(row, count), :] * value.astype(F32)
        value = value.astype(BF16)
        delta1[span(row, count), :] = value
        delta1_out[flat(row, count), :] = jnp.where(r == 0, value[:, :128], value[:, 128:])

    slope2[flat(inner(f), 6), :] = second(inner(f), 6)
    x2_in(g, 1)
    x2_in(g, 2)
    advance(x2, mid3, weights, 0, 7 - 2 * f, 4, slope1)
    slope2[flat(6, 4), :] = second(6, 4)
    remote(cotangent, adj.at[flat(own, BAND)], 5, adj_sem.at[r], (l, o)).wait_recv()

    @pl.when(even | last)
    def _():
        adj_in.wait_recv()

    turn(6 * f, 10, slope2[flat(6 * f, 10), :])
    turn_back(7 * f, 9)

    x2_in(g, 0)
    outs = [pltpu.make_async_copy(x2.at[span(0, ROWS)], states_out, out_sem.at[0])]
    outs[-1].start()
    advance(x2, mid3, weights, 0, 11 * g, 5, slope1)
    outs.append(pltpu.make_async_copy(mid3.at[span(0, ROWS)], middle_out, out_sem.at[1]))
    outs[-1].start()
    turn(10 * g, 6, second(10 * g, 6))
    turn_back(9 * g, 7)

    value = conv(delta1, weights, 0, own, BAND, back=True)
    adjoint_out[...] = (back[flat(own, BAND), :].astype(F32) + value).astype(BF16)

    halo.wait_send()
    for here, copies in (
        (first, [net1] + nets2),
        (last, [adj_last]),
        (takes, [adj_cross]),
        (odd, [adj_same]),
        (odd & passes, [adj_on] + e2_other),
        (passes, [e1_inner, e1_edge, e1_cross] + e2),
        (even, [e1_rest] + e2_same),
    ):

        @pl.when(here)
        def _(copies=copies):
            for copy in copies:
                copy.wait_send()

    for copy in outs:
        copy.wait()


def grad_kernel(
    scale,
    states, middle, delta1, delta2, adjoint,
    states_out, adjoint_out, grad_out,
    wide, grads, out_sem, grad_sem,
):
    r = lax.axis_index("rows")
    outs = [
        pltpu.make_async_copy(states.at[flat(r * BAND, BAND)], states_out, out_sem.at[0]),
        pltpu.make_async_copy(adjoint, adjoint_out, out_sem.at[1]),
    ]
    for copy in outs:
        copy.start()
    zero = jnp.zeros((W, 384), BF16)
    for layer in range(2):
        wide[layer, pl.ds(0, W), :] = zero
        wide[layer, pl.ds((ROWS + 1) * W, W), :] = zero
    col = lax.broadcasted_iota(jnp.int32, (PX, 128), 0) % W
    for layer, image, delta in ((1, middle, delta2), (0, states, delta1)):
        value = delta[...].astype(F32)
        after = jnp.where(col == W - 1, 0.0, pltpu.roll(value, PX - 1, 0))
        before = jnp.where(col == 0, 0.0, pltpu.roll(value, 1, 0))
        wide[layer, pl.ds(W, PX), 0:128] = after.astype(BF16)
        wide[layer, pl.ds(W, PX), 128:256] = delta[...]
        wide[layer, pl.ds(W, PX), 256:384] = before.astype(BF16)
        side = jnp.concatenate([wide[layer, pl.ds((2 - a) * W, PX), :] for a in range(3)], axis=1)
        for part, (low, high) in enumerate(((0, 4), (4, 8), (8, 9))):
            terms = lax.dot_general(
                image[...], side[:, low * 128 : high * 128], (((0,), (0,)), ((), ())),
                preferred_element_type=F32,
            )
            for tap in range(low, high):
                grads[layer, tap] = terms[:, (tap - low) * 128 : (tap - low + 1) * 128] * scale
            taps = pl.ds(low, high - low)
            outs.append(
                pltpu.make_async_copy(
                    grads.at[layer, taps], grad_out.at[layer, taps], grad_sem.at[layer, part]
                )
            )
            outs[-1].start()
    for copy in outs:
        copy.wait()


def solution(mesh):
    layers = mesh.shape["layer"]
    scale = 1.0 / math.sqrt(PX)
    hbm = pl.BlockSpec(memory_space=pl.ANY)
    image = lambda rows: pltpu.VMEM((rows * W, C), BF16)

    def local(guess, adj_guess, weights, net_input, cotangent):
        args = (
            guess.reshape(BPX, C),
            adj_guess.reshape(BPX, C),
            weights.reshape(18, C, C),
            net_input.reshape(BPX, C),
            cotangent.reshape(BPX, C),
        )
        sds = jax.ShapeDtypeStruct
        states, middle, delta1, delta2, adjoint = pl.pallas_call(
            lambda *refs: sweep_kernel(layers, *refs),
            out_shape=(
                pltpu.VMEM((PX, C), BF16), pltpu.VMEM((PX, C), BF16),
                pltpu.VMEM((PX, 128), BF16), pltpu.VMEM((PX, 128), BF16),
                pltpu.VMEM((BPX, C), BF16),
            ),
            in_specs=[hbm] * 5,
            out_specs=[pl.BlockSpec(memory_space=pltpu.VMEM)] * 5,
            scratch_shapes=[
                pltpu.VMEM((18, C, C), BF16),
                image(18), image(18), image(18), image(18), image(18), image(18), image(18),
                image(16), image(18), image(16), image(18),
                pltpu.VMEM((PX, C), F32),
                pltpu.VMEM((PX, C), F32),
                pltpu.SemaphoreType.DMA((3,)),
                pltpu.SemaphoreType.DMA((22,)),
                pltpu.SemaphoreType.DMA((1,)),
                pltpu.SemaphoreType.DMA((3,)),
                pltpu.SemaphoreType.DMA((2, 3)),
                pltpu.SemaphoreType.DMA((2,)),
                pltpu.SemaphoreType.DMA((2,)),
            ],
            compiler_params=pltpu.CompilerParams(
                collective_id=0, has_side_effects=True, vmem_limit_bytes=60 << 20
            ),
            name="sweeps",
        )(*args)
        states, adjoint, grads = pl.pallas_call(
            lambda *refs: grad_kernel(scale, *refs),
            out_shape=(sds((BPX, C), BF16), sds((BPX, C), BF16), sds((2, 9, C, 128), F32)),
            in_specs=[pl.BlockSpec(memory_space=pltpu.VMEM)] * 5,
            out_specs=[hbm] * 3,
            scratch_shapes=[
                pltpu.VMEM((2, 18 * W, 384), BF16),
                pltpu.VMEM((2, 9, C, 128), F32),
                pltpu.SemaphoreType.DMA((2,)),
                pltpu.SemaphoreType.DMA((2, 3)),
            ],
            compiler_params=pltpu.CompilerParams(vmem_limit_bytes=56 << 20),
            name="weight_grads",
        )(*[pltpu.with_memory_space_constraint(x, pltpu.VMEM) for x in (states, middle, delta1, delta2, adjoint)])
        shape = (1, 1, BAND, W, C)
        return states.reshape(shape), adjoint.reshape(shape), grads

    in_specs = (
        P("layer", None, "rows", None, None),
        P("layer", None, "rows", None, None),
        P("layer", None, None, None),
        P(None, "rows", None, None),
        P(None, "rows", None, None),
    )
    out_specs = (
        P("layer", None, "rows", None, None),
        P("layer", None, "rows", None, None),
        P("layer", None, None, "rows"),
    )
    return jax.shard_map(local, mesh=mesh, in_specs=in_specs, out_specs=out_specs, check_vma=False)
```

```python
import math

import jax
import jax.numpy as jnp
from jax import lax
from jax.experimental import pallas as pl
from jax.experimental.pallas import tpu as pltpu
from jax.sharding import PartitionSpec as P

MESH = pl.DeviceIdType.MESH
F32 = jnp.float32
BF16 = jnp.bfloat16
ROWS = 16
BAND = 8
W = 64
C = 256
PX = ROWS * W
BPX = BAND * W
SPLIT = 4


def span(row, count):
    start = (row + 1) * W
    return pl.ds(start if isinstance(start, int) else pl.multiple_of(start, W), count * W)


def flat(row, count):
    start = row * W
    return pl.ds(start if isinstance(start, int) else pl.multiple_of(start, W), count * W)


def conv(src, weights, layer, row, count, back=False):
    n = count * W
    shifted = []
    for b in range(3):
        acc = None
        for a in range(3):
            window = src[span(row + a - 1, count), :]
            if back:
                term = lax.dot_general(
                    window,
                    weights[layer * 9 + (2 - a) * 3 + (2 - b)],
                    (((1,), (1,)), ((), ())),
                    preferred_element_type=F32,
                )
            else:
                term = jnp.dot(window, weights[layer * 9 + a * 3 + b], preferred_element_type=F32)
            acc = term if acc is None else acc + term
        shifted.append(acc)
    col = lax.broadcasted_iota(jnp.int32, (n, C), 0) % W
    left = jnp.where(col == 0, 0.0, pltpu.roll(shifted[0], 1, 0))
    right = jnp.where(col == W - 1, 0.0, pltpu.roll(shifted[2], n - 1, 0))
    return shifted[1] + left + right


def pieces(row, count):
    low = count // 2
    return ((row, low), (row + low, count - low)) if count >= SPLIT else ((row, count),)


def sigmoid(value):
    return 1.0 / (1.0 + jnp.exp(-value))


def half_slope(value, s):
    return 0.5 * s * (1.0 + value * (1.0 - s))


def advance(src, dst, weights, layer, start, total, slope=None):
    for row, count in pieces(start, total):
        value = conv(src, weights, layer, row, count)
        s = sigmoid(value)
        state = src[span(row, count), :].astype(F32)
        dst[span(row, count), :] = (state + 0.5 * value * s).astype(BF16)
        if slope is not None:
            slope[flat(row, count), :] = half_slope(value, s)


def sweep_kernel(
    layers,
    guess, adj_guess, weights_hbm, net_input, cotangent,
    states_out, middle_out, delta1_out, delta2_out, adjoint_out,
    weights, x0, x1, x2, mid, mid3, end1, end2, adj, delta2, back, delta1, slope1, slope2,
    load_sem, ready_sem, send_sem, halo_sem, x1_sem, x2_sem, adj_sem, out_sem,
):
    l = lax.axis_index("layer")
    r = lax.axis_index("rows")
    o = 1 - r
    even = l % 2 == 0
    odd = l % 2 == 1
    first = l == 0
    last = l == layers - 1
    passes = jnp.logical_not(last)
    takes = jnp.logical_not(first)
    up = jnp.minimum(l + 1, layers - 1)
    down = jnp.maximum(l - 1, 0)
    t = (r + l) % 2
    s = jnp.where(first, r, (r + l + 1) % 2)
    own = r * BAND
    other = o * BAND

    loads = [
        pltpu.make_async_copy(guess, x0.at[span(own, BAND)], load_sem.at[0]),
        pltpu.make_async_copy(weights_hbm.at[pl.ds(0, 9)], weights.at[pl.ds(0, 9)], load_sem.at[1]),
        pltpu.make_async_copy(weights_hbm.at[pl.ds(9, 9)], weights.at[pl.ds(9, 9)], load_sem.at[2]),
    ]
    for copy in loads:
        copy.start()

    barrier = pltpu.get_barrier_semaphore()

    def greet(here, *devices):
        @pl.when(here)
        def _():
            for device in devices:
                pl.semaphore_signal(barrier, inc=1, device_id=device, device_id_type=MESH)

    greet(even & takes, (down, o))
    greet(odd & passes, (up, o))
    pl.semaphore_signal(barrier, inc=1, device_id=(l, o), device_id_type=MESH)
    greet(even, (up, r), (up, o))
    greet(odd, (down, r), (down, o))

    zero = jnp.zeros((W, C), BF16)
    for buf in (x0, x1, x2, mid, mid3, delta2, delta1):
        buf[pl.ds(0, W), :] = zero
        buf[pl.ds((ROWS + 1) * W, W), :] = zero

    @pl.when(first | last)
    def _():
        pl.semaphore_wait(barrier, 3)

    @pl.when(jnp.logical_not(first | last))
    def _():
        pl.semaphore_wait(barrier, 4)

    @pl.when(even & takes)
    def _():
        pl.semaphore_signal(ready_sem, inc=1, device_id=(down, o), device_id_type=MESH)

    def remote(src, dst, send, recv, device):
        return pltpu.make_async_remote_copy(
            src_ref=src, dst_ref=dst, send_sem=send_sem.at[send], recv_sem=recv,
            device_id=device, device_id_type=MESH,
        )

    edge = lambda band: 6 + 2 * band
    near = lambda band: 4 + 6 * band
    far = lambda band: 12 * band
    inner = lambda band: 10 * band
    parts = ((far, 4), (near, 2), (edge, 2))

    def ship(buf, target, rows, count, send, sem, device):
        return remote(buf.at[span(rows, count)], target.at[span(rows, count)], send, sem, device)

    loads[0].wait()
    halo = ship(x0, x0, edge(r), 2, 0, halo_sem.at[0], (l, o))
    halo.start()
    halo_in = ship(x0, x0, edge(o), 2, 0, halo_sem.at[0], (l, o))

    net_at = lambda rows, count: net_input.at[flat(rows - own, count)]
    net1 = remote(net_at(edge(r), 2), x1.at[span(edge(r), 2)], 1, x1_sem.at[1], (l, o))
    nets2 = [
        remote(net_at(rows(r), count), x2.at[span(rows(r), count)], 2 + part, x2_sem.at[r, part], (l, o))
        for part, (rows, count) in enumerate(parts)
    ]
    nets_here = [pltpu.make_async_copy(net_input, x1.at[span(own, BAND)], x1_sem.at[0])] + [
        pltpu.make_async_copy(net_at(rows(r), count), x2.at[span(rows(r), count)], x2_sem.at[r, part])
        for part, (rows, count) in enumerate(parts)
    ]
    adj_last = remote(cotangent, adj.at[flat(own, BAND)], 5, adj_sem.at[r], (l, o))
    adj_last_here = pltpu.make_async_copy(cotangent, adj.at[flat(own, BAND)], adj_sem.at[r])
    adj_cross = remote(adj_guess, adj.at[flat(own, BAND)], 6, adj_sem.at[r], (down, o))
    adj_same = remote(adj_guess, adj.at[flat(own, BAND)], 7, adj_sem.at[r], (down, r))

    @pl.when(first)
    def _():
        net1.start()
        for copy in nets_here:
            copy.start()

    @pl.when(takes)
    def _():
        adj_cross.start()

    @pl.when(odd)
    def _():
        adj_same.start()

    e1_inner = [
        ship(end1, x1, rows, 3, send, x1_sem.at[0], (up, t))
        for rows, send in ((13 * r, 9), (3 + 7 * r, 22))
    ]
    e1_edge = ship(end1, x1, edge(r), 2, 10, x1_sem.at[0], (up, t))
    e1_cross = ship(end1, x1, edge(r), 2, 11, x1_sem.at[1], (up, 1 - t))
    e1_rest = ship(end1, x1, inner(r), 6, 12, x1_sem.at[2], (up, o))

    loads[1].wait()
    advance(x0, mid, weights, 0, 12 * r, 4)
    loads[2].wait()
    advance(mid, end1, weights, 1, 13 * r, 3)

    @pl.when(passes)
    def _():
        e1_inner[0].start()

    advance(x0, mid, weights, 0, 4 + 5 * r, 3)
    advance(mid, end1, weights, 1, 3 + 7 * r, 3)

    @pl.when(passes)
    def _():
        e1_inner[1].start()

    halo_in.wait_recv()
    advance(x0, mid, weights, 0, 7, 2)
    advance(mid, end1, weights, 1, edge(r), 2)

    @pl.when(even)
    def _():
        e1_cross.start()
        e1_edge.start()
        e1_rest.start()

    @pl.when(odd & passes)
    def _():
        e1_edge.start()
        pl.semaphore_wait(ready_sem, 1)
        e1_cross.start()

    @pl.when(last)
    def _():
        adj_last.start()
        adj_last_here.start()

    adj_in = remote(adj_guess, adj.at[flat(other, BAND)], 6, adj_sem.at[o], (l, o))
    adj_on = remote(adj.at[flat(other, BAND)], adj.at[flat(other, BAND)], 8, adj_sem.at[o], (l, o))

    e2 = [
        ship(end2, x2, rows(s), count, 13 + part, x2_sem.at[s, part], (up, o))
        for part, (rows, count) in enumerate(parts)
    ]
    e2_same = [
        ship(end2, x2, rows(s), count, 16 + part, x2_sem.at[s, part], (up, r))
        for part, (rows, count) in enumerate(parts)
    ]

    q = 1 - s
    x1_own = ship(end1, x1, s * BAND, BAND, 9, x1_sem.at[0], (l, o))
    x1_edge = ship(end1, x1, edge(q), 2, 11, x1_sem.at[1], (l, o))
    x1_rest = ship(end1, x1, inner(q), 6, 12, x1_sem.at[2], (l, o))
    e2_other = [
        ship(end2, x2, rows(q), count, 19 + part, x2_sem.at[q, part], (up, o))
        for part, (rows, count) in enumerate(parts)
    ]

    distant = l % 16 == 15

    def pass_adjoint(here):
        @pl.when(here & passes)
        def _():
            adj_in.wait_recv()
            adj_on.start()

    @pl.when(even)
    def _():
        x1_own.wait_recv()
        x1_edge.wait_recv()
        advance(x1, mid, weights, 0, 7 * s, 9)
        advance(mid, end2, weights, 1, s * BAND, BAND)

        @pl.when(first)
        def _():
            nets2[2].start()
            nets2[1].start()

        for part in (2, 1, 0):
            e2_same[part].start()
            e2[part].start()

        @pl.when(first)
        def _():
            nets2[0].start()

    @pl.when(odd)
    def _():
        x1_own.wait_recv()
        advance(x1, mid, weights, 0, 9 * s, 7)
        advance(mid, end2, weights, 1, inner(s), 6)

        @pl.when(passes)
        def _():
            e2[0].start()
            e2[1].start()

        x1_edge.wait_recv()
        advance(x1, mid, weights, 0, 7, 2)
        advance(mid, end2, weights, 1, edge(s), 2)

        @pl.when(passes)
        def _():
            e2[2].start()

        pass_adjoint(jnp.logical_not(distant))
        x1_rest.wait_recv()

        @pl.when(passes)
        def _():
            advance(x1, mid, weights, 0, 3 + 6 * q, 4)
            advance(mid, end2, weights, 1, 4 + 4 * q, 4)
            for copy in e2_other[1:]:
                copy.start()

        pass_adjoint(distant)

        @pl.when(passes)
        def _():
            advance(x1, mid, weights, 0, 13 * q, 3)
            advance(mid, end2, weights, 1, far(q), 4)
            e2_other[0].start()

    x2_in = lambda band, part: ship(
        end2, x2, parts[part][0](band), parts[part][1], 13, x2_sem.at[band, part], (l, o)
    ).wait_recv()
    f = jnp.where(l < 2, r, o)
    g = 1 - f
    for part in range(3):
        x2_in(f, part)
    advance(x2, mid3, weights, 0, 9 * f, 7, slope1)

    def second(start, total, then=None):
        for row, count in pieces(start, total):
            value = conv(mid3, weights, 1, row, count)
            value = half_slope(value, sigmoid(value))
            if then is None:
                slope2[flat(row, count), :] = value
            else:
                then(row, count, value)

    def turn(row, count, slope):
        value = (slope * adj[flat(row, count), :].astype(F32)).astype(BF16)
        delta2[span(row, count), :] = value
        delta2_out[flat(row, count), :] = jnp.where(r == 0, value[:, :128], value[:, 128:])

    def turn_back(start, total):
        for row, count in pieces(start, total):
            value = conv(delta2, weights, 1, row, count, back=True)
            value = (adj[flat(row, count), :].astype(F32) + value).astype(BF16)
            back[flat(row, count), :] = value
            value = (slope1[flat(row, count), :] * value.astype(F32)).astype(BF16)
            delta1[span(row, count), :] = value
            delta1_out[flat(row, count), :] = jnp.where(r == 0, value[:, :128], value[:, 128:])

    second(inner(f), 6)
    x2_in(g, 1)
    x2_in(g, 2)
    advance(x2, mid3, weights, 0, 7 - 2 * f, 4, slope1)
    second(6, 4)
    remote(cotangent, adj.at[flat(own, BAND)], 5, adj_sem.at[r], (l, o)).wait_recv()

    @pl.when(even | last)
    def _():
        adj_in.wait_recv()

    turn(6 * f, 10, slope2[flat(6 * f, 10), :])
    turn_back(7 * f, 9)

    x2_in(g, 0)
    outs = [pltpu.make_async_copy(x2.at[span(0, ROWS)], states_out, out_sem.at[0])]
    outs[-1].start()
    advance(x2, mid3, weights, 0, 11 * g, 5, slope1)
    outs.append(pltpu.make_async_copy(mid3.at[span(0, ROWS)], middle_out, out_sem.at[1]))
    outs[-1].start()
    second(10 * g, 6, turn)
    turn_back(9 * g, 7)

    for row, count in pieces(own, BAND):
        value = conv(delta1, weights, 0, row, count, back=True)
        at = flat(row - own, count)
        adjoint_out[at, :] = (back[flat(row, count), :].astype(F32) + value).astype(BF16)

    halo.wait_send()
    for here, copies in (
        (first, [net1] + nets2),
        (last, [adj_last]),
        (takes, [adj_cross]),
        (odd, [adj_same]),
        (odd & passes, [adj_on] + e2_other),
        (passes, e1_inner + [e1_edge, e1_cross] + e2),
        (even, [e1_rest] + e2_same),
    ):

        @pl.when(here)
        def _(copies=copies):
            for copy in copies:
                copy.wait_send()

    for copy in outs:
        copy.wait()


def grad_kernel(
    scale,
    states, middle, delta1, delta2, adjoint,
    states_out, adjoint_out, grad_out,
    wide, grads, out_sem, grad_sem,
):
    r = lax.axis_index("rows")
    outs = [
        pltpu.make_async_copy(states.at[flat(r * BAND, BAND)], states_out, out_sem.at[0]),
        pltpu.make_async_copy(adjoint, adjoint_out, out_sem.at[1]),
    ]
    for copy in outs:
        copy.start()
    zero = jnp.zeros((W, 384), BF16)
    for layer in range(2):
        wide[layer, pl.ds(0, W), :] = zero
        wide[layer, pl.ds((ROWS + 1) * W, W), :] = zero
    col = lax.broadcasted_iota(jnp.int32, (PX, 128), 0) % W
    for layer, image, delta in ((1, middle, delta2), (0, states, delta1)):
        value = delta[...].astype(F32)
        after = jnp.where(col == W - 1, 0.0, pltpu.roll(value, PX - 1, 0))
        before = jnp.where(col == 0, 0.0, pltpu.roll(value, 1, 0))
        wide[layer, pl.ds(W, PX), 0:128] = after.astype(BF16)
        wide[layer, pl.ds(W, PX), 128:256] = delta[...]
        wide[layer, pl.ds(W, PX), 256:384] = before.astype(BF16)
        side = jnp.concatenate([wide[layer, pl.ds((2 - a) * W, PX), :] for a in range(3)], axis=1)
        for part, (low, high) in enumerate(((0, 4), (4, 8), (8, 9))):
            terms = lax.dot_general(
                image[...], side[:, low * 128 : high * 128], (((0,), (0,)), ((), ())),
                preferred_element_type=F32,
            )
            for tap in range(low, high):
                grads[layer, tap] = terms[:, (tap - low) * 128 : (tap - low + 1) * 128] * scale
            taps = pl.ds(low, high - low)
            outs.append(
                pltpu.make_async_copy(
                    grads.at[layer, taps], grad_out.at[layer, taps], grad_sem.at[layer, part]
                )
            )
            outs[-1].start()
    for copy in outs:
        copy.wait()


def solution(mesh):
    layers = mesh.shape["layer"]
    scale = 1.0 / math.sqrt(PX)
    hbm = pl.BlockSpec(memory_space=pl.ANY)
    image = lambda rows: pltpu.VMEM((rows * W, C), BF16)

    def local(guess, adj_guess, weights, net_input, cotangent):
        args = (
            guess.reshape(BPX, C),
            adj_guess.reshape(BPX, C),
            weights.reshape(18, C, C),
            net_input.reshape(BPX, C),
            cotangent.reshape(BPX, C),
        )
        sds = jax.ShapeDtypeStruct
        states, middle, delta1, delta2, adjoint = pl.pallas_call(
            lambda *refs: sweep_kernel(layers, *refs),
            out_shape=(
                pltpu.VMEM((PX, C), BF16), pltpu.VMEM((PX, C), BF16),
                pltpu.VMEM((PX, 128), BF16), pltpu.VMEM((PX, 128), BF16),
                pltpu.VMEM((BPX, C), BF16),
            ),
            in_specs=[hbm] * 5,
            out_specs=[pl.BlockSpec(memory_space=pltpu.VMEM)] * 5,
            scratch_shapes=[
                pltpu.VMEM((18, C, C), BF16),
                image(18), image(18), image(18), image(18), image(18), image(18), image(18),
                image(16), image(18), image(16), image(18),
                pltpu.VMEM((PX, C), F32),
                pltpu.VMEM((PX, C), F32),
                pltpu.SemaphoreType.DMA((3,)),
                pltpu.SemaphoreType.REGULAR,
                pltpu.SemaphoreType.DMA((23,)),
                pltpu.SemaphoreType.DMA((1,)),
                pltpu.SemaphoreType.DMA((3,)),
                pltpu.SemaphoreType.DMA((2, 3)),
                pltpu.SemaphoreType.DMA((2,)),
                pltpu.SemaphoreType.DMA((2,)),
            ],
            compiler_params=pltpu.CompilerParams(
                collective_id=0, has_side_effects=True, vmem_limit_bytes=60 << 20
            ),
            name="sweeps",
        )(*args)
        states, adjoint, grads = pl.pallas_call(
            lambda *refs: grad_kernel(scale, *refs),
            out_shape=(sds((BPX, C), BF16), sds((BPX, C), BF16), sds((2, 9, C, 128), F32)),
            in_specs=[pl.BlockSpec(memory_space=pltpu.VMEM)] * 5,
            out_specs=[hbm] * 3,
            scratch_shapes=[
                pltpu.VMEM((2, 18 * W, 384), BF16),
                pltpu.VMEM((2, 9, C, 128), F32),
                pltpu.SemaphoreType.DMA((2,)),
                pltpu.SemaphoreType.DMA((2, 3)),
            ],
            compiler_params=pltpu.CompilerParams(vmem_limit_bytes=56 << 20),
            name="weight_grads",
        )(*[pltpu.with_memory_space_constraint(x, pltpu.VMEM) for x in (states, middle, delta1, delta2, adjoint)])
        shape = (1, 1, BAND, W, C)
        return states.reshape(shape), adjoint.reshape(shape), grads

    in_specs = (
        P("layer", None, "rows", None, None),
        P("layer", None, "rows", None, None),
        P("layer", None, None, None),
        P(None, "rows", None, None),
        P(None, "rows", None, None),
    )
    out_specs = (
        P("layer", None, "rows", None, None),
        P("layer", None, "rows", None, None),
        P("layer", None, None, "rows"),
    )
    return jax.shard_map(local, mesh=mesh, in_specs=in_specs, out_specs=out_specs, check_vma=False)
```

```python
import math

import jax
import jax.numpy as jnp
from jax import lax
from jax.experimental import pallas as pl
from jax.experimental.pallas import tpu as pltpu
from jax.sharding import PartitionSpec as P

MESH = pl.DeviceIdType.MESH
F32 = jnp.float32
BF16 = jnp.bfloat16
ROWS = 16
BAND = 8
W = 64
C = 256
PX = ROWS * W
BPX = BAND * W
SPLIT = 4


def span(row, count):
    start = (row + 1) * W
    return pl.ds(start if isinstance(start, int) else pl.multiple_of(start, W), count * W)


def flat(row, count):
    start = row * W
    return pl.ds(start if isinstance(start, int) else pl.multiple_of(start, W), count * W)


def conv(src, weights, layer, row, count, back=False):
    n = count * W
    shifted = []
    for b in range(3):
        acc = None
        for a in range(3):
            window = src[span(row + a - 1, count), :]
            if back:
                term = lax.dot_general(
                    window,
                    weights[layer * 9 + (2 - a) * 3 + (2 - b)],
                    (((1,), (1,)), ((), ())),
                    preferred_element_type=F32,
                )
            else:
                term = jnp.dot(window, weights[layer * 9 + a * 3 + b], preferred_element_type=F32)
            acc = term if acc is None else acc + term
        shifted.append(acc)
    col = lax.broadcasted_iota(jnp.int32, (n, C), 0) % W
    left = jnp.where(col == 0, 0.0, pltpu.roll(shifted[0], 1, 0))
    right = jnp.where(col == W - 1, 0.0, pltpu.roll(shifted[2], n - 1, 0))
    return shifted[1] + left + right


def pieces(row, count):
    low = count // 2
    return ((row, low), (row + low, count - low)) if count >= SPLIT else ((row, count),)


def sigmoid(value):
    return 1.0 / (1.0 + jnp.exp(-value))


def half_slope(value, s):
    return 0.5 * s * (1.0 + value * (1.0 - s))


def advance(src, dst, weights, layer, start, total, slope=None):
    for row, count in pieces(start, total):
        value = conv(src, weights, layer, row, count)
        s = sigmoid(value)
        state = src[span(row, count), :].astype(F32)
        dst[span(row, count), :] = (state + 0.5 * value * s).astype(BF16)
        if slope is not None:
            slope[flat(row, count), :] = half_slope(value, s)


def sweep_kernel(
    layers,
    guess, adj_guess, weights_hbm, net_input, cotangent,
    states_out, middle_out, delta1_out, delta2_out, adjoint_out,
    weights, x0, x1, x2, mid, mid3, end1, end2, adj, delta2, back, delta1, slope1, slope2,
    load_sem, ready_sem, send_sem, halo_sem, x1_sem, x2_sem, adj_sem, out_sem,
):
    l = lax.axis_index("layer")
    r = lax.axis_index("rows")
    o = 1 - r
    even = l % 2 == 0
    odd = l % 2 == 1
    first = l == 0
    last = l == layers - 1
    passes = jnp.logical_not(last)
    takes = jnp.logical_not(first)
    up = jnp.minimum(l + 1, layers - 1)
    down = jnp.maximum(l - 1, 0)
    t = (r + l) % 2
    s = jnp.where(first, r, (r + l + 1) % 2)
    own = r * BAND
    other = o * BAND

    loads = [
        pltpu.make_async_copy(guess, x0.at[span(own, BAND)], load_sem.at[0]),
        pltpu.make_async_copy(weights_hbm.at[pl.ds(0, 9)], weights.at[pl.ds(0, 9)], load_sem.at[1]),
        pltpu.make_async_copy(weights_hbm.at[pl.ds(9, 9)], weights.at[pl.ds(9, 9)], load_sem.at[2]),
    ]
    for copy in loads:
        copy.start()

    barrier = pltpu.get_barrier_semaphore()

    def greet(here, *devices):
        @pl.when(here)
        def _():
            for device in devices:
                pl.semaphore_signal(barrier, inc=1, device_id=device, device_id_type=MESH)

    greet(even & takes, (down, o))
    greet(odd & passes, (up, o))
    pl.semaphore_signal(barrier, inc=1, device_id=(l, o), device_id_type=MESH)
    greet(even, (up, r), (up, o))
    greet(odd, (down, r), (down, o))

    zero = jnp.zeros((W, C), BF16)
    for buf in (x0, x1, x2, mid, mid3, delta2, delta1):
        buf[pl.ds(0, W), :] = zero
        buf[pl.ds((ROWS + 1) * W, W), :] = zero

    @pl.when(first | last)
    def _():
        pl.semaphore_wait(barrier, 3)

    @pl.when(jnp.logical_not(first | last))
    def _():
        pl.semaphore_wait(barrier, 4)

    @pl.when(even & takes)
    def _():
        pl.semaphore_signal(ready_sem, inc=1, device_id=(down, o), device_id_type=MESH)

    def remote(src, dst, send, recv, device):
        return pltpu.make_async_remote_copy(
            src_ref=src, dst_ref=dst, send_sem=send_sem.at[send], recv_sem=recv,
            device_id=device, device_id_type=MESH,
        )

    edge = lambda band: 6 + 2 * band
    near = lambda band: 4 + 6 * band
    far = lambda band: 12 * band
    inner = lambda band: 10 * band
    parts = ((far, 4), (near, 2), (edge, 2))

    def ship(buf, target, rows, count, send, sem, device):
        return remote(buf.at[span(rows, count)], target.at[span(rows, count)], send, sem, device)

    loads[0].wait()
    halo = ship(x0, x0, edge(r), 2, 0, halo_sem.at[0], (l, o))
    halo.start()
    halo_in = ship(x0, x0, edge(o), 2, 0, halo_sem.at[0], (l, o))

    net_at = lambda rows, count: net_input.at[flat(rows - own, count)]
    net1 = remote(net_at(edge(r), 2), x1.at[span(edge(r), 2)], 1, x1_sem.at[1], (l, o))
    nets2 = [
        remote(net_at(rows(r), count), x2.at[span(rows(r), count)], 2 + part, x2_sem.at[r, part], (l, o))
        for part, (rows, count) in enumerate(parts)
    ]
    nets_here = [pltpu.make_async_copy(net_input, x1.at[span(own, BAND)], x1_sem.at[0])] + [
        pltpu.make_async_copy(net_at(rows(r), count), x2.at[span(rows(r), count)], x2_sem.at[r, part])
        for part, (rows, count) in enumerate(parts)
    ]
    adj_last = remote(cotangent, adj.at[flat(own, BAND)], 5, adj_sem.at[r], (l, o))
    adj_last_here = pltpu.make_async_copy(cotangent, adj.at[flat(own, BAND)], adj_sem.at[r])
    adj_cross = remote(adj_guess, adj.at[flat(own, BAND)], 6, adj_sem.at[r], (down, o))
    adj_same = remote(adj_guess, adj.at[flat(own, BAND)], 7, adj_sem.at[r], (down, r))

    @pl.when(first)
    def _():
        net1.start()
        for copy in nets_here:
            copy.start()

    @pl.when(takes)
    def _():
        adj_cross.start()

    @pl.when(odd)
    def _():
        adj_same.start()

    e1_inner = [
        ship(end1, x1, rows, 3, send, x1_sem.at[0], (up, t))
        for rows, send in ((13 * r, 9), (3 + 7 * r, 22))
    ]
    e1_edge = ship(end1, x1, edge(r), 2, 10, x1_sem.at[0], (up, t))
    e1_cross = ship(end1, x1, edge(r), 2, 11, x1_sem.at[1], (up, 1 - t))
    e1_rest = [
        ship(end1, x1, 2 + 8 * r, 4, 12, x1_sem.at[2], (up, o)),
        ship(end1, x1, 14 * r, 2, 23, x1_sem.at[3], (up, o)),
    ]

    loads[1].wait()
    advance(x0, mid, weights, 0, 12 * r, 4)
    loads[2].wait()
    advance(mid, end1, weights, 1, 13 * r, 3)

    @pl.when(passes)
    def _():
        e1_inner[0].start()

    advance(x0, mid, weights, 0, 4 + 5 * r, 3)
    advance(mid, end1, weights, 1, 3 + 7 * r, 3)

    @pl.when(passes)
    def _():
        e1_inner[1].start()

    halo_in.wait_recv()
    advance(x0, mid, weights, 0, 7, 2)
    advance(mid, end1, weights, 1, edge(r), 2)

    @pl.when(even)
    def _():
        e1_cross.start()
        e1_edge.start()
        for copy in e1_rest:
            copy.start()

    @pl.when(odd & passes)
    def _():
        e1_edge.start()
        pl.semaphore_wait(ready_sem, 1)
        e1_cross.start()

    @pl.when(last)
    def _():
        adj_last.start()
        adj_last_here.start()

    adj_in = remote(adj_guess, adj.at[flat(other, BAND)], 6, adj_sem.at[o], (l, o))
    adj_on = remote(adj.at[flat(other, BAND)], adj.at[flat(other, BAND)], 8, adj_sem.at[o], (l, o))

    e2 = [
        ship(end2, x2, rows(s), count, 13 + part, x2_sem.at[s, part], (up, o))
        for part, (rows, count) in enumerate(parts)
    ]
    e2_same = [
        ship(end2, x2, rows(s), count, 16 + part, x2_sem.at[s, part], (up, r))
        for part, (rows, count) in enumerate(parts)
    ]

    q = 1 - s
    x1_own = ship(end1, x1, s * BAND, BAND, 9, x1_sem.at[0], (l, o))
    x1_edge = ship(end1, x1, edge(q), 2, 11, x1_sem.at[1], (l, o))
    x1_rest = [
        ship(end1, x1, 2 + 8 * q, 4, 12, x1_sem.at[2], (l, o)),
        ship(end1, x1, 14 * q, 2, 23, x1_sem.at[3], (l, o)),
    ]
    e2_other = [
        ship(end2, x2, rows(q), count, 19 + part, x2_sem.at[q, part], (up, o))
        for part, (rows, count) in enumerate(parts)
    ]

    distant = l % 16 == 15

    def pass_adjoint(here):
        @pl.when(here & passes)
        def _():
            adj_in.wait_recv()
            adj_on.start()

    @pl.when(even)
    def _():
        x1_own.wait_recv()
        x1_edge.wait_recv()
        advance(x1, mid, weights, 0, 7 * s, 9)
        advance(mid, end2, weights, 1, s * BAND, BAND)

        @pl.when(first)
        def _():
            nets2[2].start()
            nets2[1].start()

        for copy in (e2[2], e2[1], e2_same[2], e2_same[1], e2_same[0], e2[0]):
            copy.start()

        @pl.when(first)
        def _():
            nets2[0].start()

    @pl.when(odd)
    def _():
        x1_own.wait_recv()
        advance(x1, mid, weights, 0, 9 * s, 7)
        advance(mid, end2, weights, 1, inner(s), 6)

        @pl.when(passes)
        def _():
            e2[0].start()
            e2[1].start()

        x1_edge.wait_recv()
        advance(x1, mid, weights, 0, 7, 2)
        advance(mid, end2, weights, 1, edge(s), 2)

        @pl.when(passes)
        def _():
            e2[2].start()

        pass_adjoint(jnp.logical_not(distant))
        x1_rest[0].wait_recv()

        @pl.when(passes)
        def _():
            advance(x1, mid, weights, 0, 3 + 6 * q, 4)
            advance(mid, end2, weights, 1, 4 + 4 * q, 4)
            for copy in e2_other[1:]:
                copy.start()

        pass_adjoint(distant)
        x1_rest[1].wait_recv()

        @pl.when(passes)
        def _():
            advance(x1, mid, weights, 0, 13 * q, 3)
            advance(mid, end2, weights, 1, far(q), 4)
            e2_other[0].start()

    x2_in = lambda band, part: ship(
        end2, x2, parts[part][0](band), parts[part][1], 13, x2_sem.at[band, part], (l, o)
    ).wait_recv()
    f = jnp.where(l < 2, r, o)
    g = 1 - f
    for part in range(3):
        x2_in(f, part)
    advance(x2, mid3, weights, 0, 9 * f, 7, slope1)

    def second(start, total, then=None):
        for row, count in pieces(start, total):
            value = conv(mid3, weights, 1, row, count)
            value = half_slope(value, sigmoid(value))
            if then is None:
                slope2[flat(row, count), :] = value
            else:
                then(row, count, value)

    def turn(row, count, slope):
        value = (slope * adj[flat(row, count), :].astype(F32)).astype(BF16)
        delta2[span(row, count), :] = value
        delta2_out[flat(row, count), :] = jnp.where(r == 0, value[:, :128], value[:, 128:])

    def turn_back(start, total):
        for row, count in pieces(start, total):
            value = conv(delta2, weights, 1, row, count, back=True)
            value = (adj[flat(row, count), :].astype(F32) + value).astype(BF16)
            back[flat(row, count), :] = value
            value = (slope1[flat(row, count), :] * value.astype(F32)).astype(BF16)
            delta1[span(row, count), :] = value
            delta1_out[flat(row, count), :] = jnp.where(r == 0, value[:, :128], value[:, 128:])

    second(inner(f), 6)
    x2_in(g, 1)
    x2_in(g, 2)
    advance(x2, mid3, weights, 0, 7 - 2 * f, 4, slope1)
    second(6, 4)
    remote(cotangent, adj.at[flat(own, BAND)], 5, adj_sem.at[r], (l, o)).wait_recv()

    @pl.when(even | last)
    def _():
        adj_in.wait_recv()

    turn(6 * f, 10, slope2[flat(6 * f, 10), :])
    turn_back(7 * f, 9)

    x2_in(g, 0)
    outs = [pltpu.make_async_copy(x2.at[span(0, ROWS)], states_out, out_sem.at[0])]
    outs[-1].start()
    advance(x2, mid3, weights, 0, 11 * g, 5, slope1)
    outs.append(pltpu.make_async_copy(mid3.at[span(0, ROWS)], middle_out, out_sem.at[1]))
    outs[-1].start()
    second(10 * g, 6, turn)
    turn_back(9 * g, 7)

    for row, count in pieces(own, BAND):
        value = conv(delta1, weights, 0, row, count, back=True)
        at = flat(row - own, count)
        adjoint_out[at, :] = (back[flat(row, count), :].astype(F32) + value).astype(BF16)

    halo.wait_send()
    for here, copies in (
        (first, [net1] + nets2),
        (last, [adj_last]),
        (takes, [adj_cross]),
        (odd, [adj_same]),
        (odd & passes, [adj_on] + e2_other),
        (passes, e1_inner + [e1_edge, e1_cross] + e2),
        (even, e1_rest + e2_same),
    ):

        @pl.when(here)
        def _(copies=copies):
            for copy in copies:
                copy.wait_send()

    for copy in outs:
        copy.wait()


def grad_kernel(
    scale,
    states, middle, delta1, delta2, adjoint,
    states_out, adjoint_out, grad_out,
    wide, grads, out_sem, grad_sem,
):
    r = lax.axis_index("rows")
    outs = [
        pltpu.make_async_copy(states.at[flat(r * BAND, BAND)], states_out, out_sem.at[0]),
        pltpu.make_async_copy(adjoint, adjoint_out, out_sem.at[1]),
    ]
    for copy in outs:
        copy.start()
    zero = jnp.zeros((W, 384), BF16)
    for layer in range(2):
        wide[layer, pl.ds(0, W), :] = zero
        wide[layer, pl.ds((ROWS + 1) * W, W), :] = zero
    col = lax.broadcasted_iota(jnp.int32, (PX, 128), 0) % W
    for layer, image, delta in ((1, middle, delta2), (0, states, delta1)):
        value = delta[...].astype(F32)
        after = jnp.where(col == W - 1, 0.0, pltpu.roll(value, PX - 1, 0))
        before = jnp.where(col == 0, 0.0, pltpu.roll(value, 1, 0))
        wide[layer, pl.ds(W, PX), 0:128] = after.astype(BF16)
        wide[layer, pl.ds(W, PX), 128:256] = delta[...]
        wide[layer, pl.ds(W, PX), 256:384] = before.astype(BF16)
        side = jnp.concatenate([wide[layer, pl.ds((2 - a) * W, PX), :] for a in range(3)], axis=1)
        for part, (low, high) in enumerate(((0, 4), (4, 8), (8, 9))):
            terms = lax.dot_general(
                image[...], side[:, low * 128 : high * 128], (((0,), (0,)), ((), ())),
                preferred_element_type=F32,
            )
            for tap in range(low, high):
                grads[layer, tap] = terms[:, (tap - low) * 128 : (tap - low + 1) * 128] * scale
            taps = pl.ds(low, high - low)
            outs.append(
                pltpu.make_async_copy(
                    grads.at[layer, taps], grad_out.at[layer, taps], grad_sem.at[layer, part]
                )
            )
            outs[-1].start()
    for copy in outs:
        copy.wait()


def solution(mesh):
    layers = mesh.shape["layer"]
    scale = 1.0 / math.sqrt(PX)
    hbm = pl.BlockSpec(memory_space=pl.ANY)
    image = lambda rows: pltpu.VMEM((rows * W, C), BF16)

    def local(guess, adj_guess, weights, net_input, cotangent):
        args = (
            guess.reshape(BPX, C),
            adj_guess.reshape(BPX, C),
            weights.reshape(18, C, C),
            net_input.reshape(BPX, C),
            cotangent.reshape(BPX, C),
        )
        sds = jax.ShapeDtypeStruct
        states, middle, delta1, delta2, adjoint = pl.pallas_call(
            lambda *refs: sweep_kernel(layers, *refs),
            out_shape=(
                pltpu.VMEM((PX, C), BF16), pltpu.VMEM((PX, C), BF16),
                pltpu.VMEM((PX, 128), BF16), pltpu.VMEM((PX, 128), BF16),
                pltpu.VMEM((BPX, C), BF16),
            ),
            in_specs=[hbm] * 5,
            out_specs=[pl.BlockSpec(memory_space=pltpu.VMEM)] * 5,
            scratch_shapes=[
                pltpu.VMEM((18, C, C), BF16),
                image(18), image(18), image(18), image(18), image(18), image(18), image(18),
                image(16), image(18), image(16), image(18),
                pltpu.VMEM((PX, C), F32),
                pltpu.VMEM((PX, C), F32),
                pltpu.SemaphoreType.DMA((3,)),
                pltpu.SemaphoreType.REGULAR,
                pltpu.SemaphoreType.DMA((24,)),
                pltpu.SemaphoreType.DMA((1,)),
                pltpu.SemaphoreType.DMA((4,)),
                pltpu.SemaphoreType.DMA((2, 3)),
                pltpu.SemaphoreType.DMA((2,)),
                pltpu.SemaphoreType.DMA((2,)),
            ],
            compiler_params=pltpu.CompilerParams(
                collective_id=0, has_side_effects=True, vmem_limit_bytes=60 << 20
            ),
            name="sweeps",
        )(*args)
        states, adjoint, grads = pl.pallas_call(
            lambda *refs: grad_kernel(scale, *refs),
            out_shape=(sds((BPX, C), BF16), sds((BPX, C), BF16), sds((2, 9, C, 128), F32)),
            in_specs=[pl.BlockSpec(memory_space=pltpu.VMEM)] * 5,
            out_specs=[hbm] * 3,
            scratch_shapes=[
                pltpu.VMEM((2, 18 * W, 384), BF16),
                pltpu.VMEM((2, 9, C, 128), F32),
                pltpu.SemaphoreType.DMA((2,)),
                pltpu.SemaphoreType.DMA((2, 3)),
            ],
            compiler_params=pltpu.CompilerParams(vmem_limit_bytes=56 << 20),
            name="weight_grads",
        )(*[pltpu.with_memory_space_constraint(x, pltpu.VMEM) for x in (states, middle, delta1, delta2, adjoint)])
        shape = (1, 1, BAND, W, C)
        return states.reshape(shape), adjoint.reshape(shape), grads

    in_specs = (
        P("layer", None, "rows", None, None),
        P("layer", None, "rows", None, None),
        P("layer", None, None, None),
        P(None, "rows", None, None),
        P(None, "rows", None, None),
    )
    out_specs = (
        P("layer", None, "rows", None, None),
        P("layer", None, "rows", None, None),
        P("layer", None, None, "rows"),
    )
    return jax.shard_map(local, mesh=mesh, in_specs=in_specs, out_specs=out_specs, check_vma=False)
```
